512 devices in a mesh: mem: 16 (over z_lo, core), lat: 32 (over x, y, z_hi).
Axes of the slice: x: 4, y: 4, z: 16 (z_hi: 2, z_lo: 8; z = z_hi * 8 + z_lo), core: 2. Of those that a mesh axis runs over, the one named last changes fastest.
Arguments:
- control: bfloat16 [32, 10, 704, 1440], P('mem', None, 'lat'), may hold values from -6 to 6
- perturb: bfloat16 [32, 10, 704, 1440], P('mem', None, None, 'lat'), may hold values from -6 to 6
- lon_loc: bfloat16 [1440, 1440], P(None, 'mem'), may hold values from 0 to 1, as said below
- lat_loc: bfloat16 [704, 704], P('mem'), may hold values from 0 to 1, as said below
- static_scale: float32 [10, 704, 1440], P(None, 'mem', 'lat'), may hold values from 0.3 to 1
- static_field: float32 [10, 704, 1440], P(None, 'mem', 'lat'), may hold values from -6 to 6
- courant: float32 [2, 704, 1440], P(None, 'mem', 'lat'), may hold values from -0.48 to 0.48
Outputs:
- increment: float32 [10, 704, 1440], P(None, 'mem', 'lat')
- evolved: float32 [10, 704, 1440], P(None, 'mem', 'lat')
The draws below stay inside these ranges and needn't reach their ends.
Inputs may be any that keep to these rules, and one draw needn't show every extreme that they name: `lon_loc`: Symmetric, with positive entries. `lat_loc`: Symmetric, with positive entries.
All inputs are finite; a program needn't handle non-finite values.
Results may differ from the reference program's by a relative error of at most 0.0027.
Values may be sent and summed in bfloat16 or wider, within the bound.
A program may use at most 64 MiB of HBM per device.

```python
import math
import jax
import jax.numpy as jnp
from jax import lax

MEMBERS = 32
FIELDS = 10
NLAT = 704
NLON = 1440
STEPS = 4


def gaussian_taper(key, amount, periodic):
    cells = jnp.arange(amount, dtype=jnp.int32)
    distance = jnp.abs(cells[:, None] - cells[None, :])
    if periodic:
        distance = jnp.minimum(distance, amount - distance)
    length = amount / 32.0
    floor_level = 0.15
    spacing = distance.astype(jnp.float32)
    envelope = floor_level + (1.0 - floor_level) * jnp.exp(-(spacing * spacing) / (2.0 * length * length))
    modulation = jax.random.uniform(key, (amount, amount), jnp.float32, 0.5, 1.5)
    symmetric = 0.5 * (modulation + modulation.T)
    normalizer = jnp.sqrt(amount * floor_level * floor_level + length * 1.7725)
    return (envelope * symmetric / normalizer).astype(jnp.bfloat16)


def draw_lon_loc(key, part):
    return gaussian_taper(jax.random.fold_in(key, 11), NLON, True)


def draw_lat_loc(key, part):
    return gaussian_taper(jax.random.fold_in(key, 23), NLAT, False)


def raised(array, rng, source, target, blocks, factor):
    def block_of(position):
        return (jnp.arange(array.shape[position]) // (array.shape[position] // blocks)).reshape((-1,) + (1,) * (array.ndim - 1 - position))

    first = jax.random.permutation(rng, blocks)[block_of(target)]
    far = (block_of(target) + blocks // 2) % blocks
    return jnp.where((block_of(source) == first) | (block_of(source) == far), factor * array, array)


def steps_of(key, extent, shards, least, largest):
    loudness = 1.0
    for dim, parts in shards:
        heights = jax.random.uniform(jax.random.fold_in(jax.random.fold_in(key, 6), dim), (parts,), jnp.float32, least / len(shards), largest / len(shards))
        loudness = loudness * jnp.repeat(jnp.exp(heights), extent[dim] // parts).reshape((-1,) + (1,) * (len(extent) - 1 - dim))
    return loudness


def scatter_about(own_key, extent, scale, bound, cuts=(), held_as=jnp.bfloat16):
    values = jax.random.normal(own_key, extent, jnp.float32) * scale
    if len(cuts) > 0:
        values = steps_of(own_key, extent, cuts, -0.22, 0.18) * values
    return jnp.clip(values, min=-bound, max=bound).astype(held_as)


def gaussian_with(rng, dims, spread, limit, shards, heavy, held_as=jnp.bfloat16):
    entries = spread * jax.random.normal(rng, dims, jnp.float32)
    if shards:
        entries = entries * steps_of(rng, dims, shards, -0.22, 0.18)
    return jnp.clip(raised(entries, jax.random.fold_in(rng, 3), *heavy), -limit, limit).astype(held_as)


def setup_inputs(seed: int = 0) -> dict:
    arg_keys = jax.random.split(jax.random.key(seed), 8)
    return {
        "control": scatter_about(arg_keys[0], (MEMBERS, FIELDS, NLAT, NLON), 1.0, 6.0, ((0, 16), (2, 32))),
        "perturb": gaussian_with(arg_keys[1], (MEMBERS, FIELDS, NLAT, NLON), 1.0, 6.0, ((0, 16), (3, 32)), (0, 2, 16, 2.0)),
        "lon_loc": draw_lon_loc(jax.random.fold_in(arg_keys[7], 71), 0),
        "lat_loc": draw_lat_loc(jax.random.fold_in(arg_keys[7], 71), 0),
        "static_scale": jnp.clip(jnp.exp(math.log(1.0) - 1.2039728 * jax.random.uniform(arg_keys[4], (FIELDS, NLAT, NLON), jnp.float32) ** steps_of(arg_keys[4], (FIELDS, NLAT, NLON), ((1, 16), (2, 32)), -0.2, 0.2)), 0.3, 1.0),
        "static_field": scatter_about(arg_keys[5], (FIELDS, NLAT, NLON), 1.0, 6.0, ((1, 16), (2, 32)), jnp.float32),
        "courant": jnp.clip(jax.random.uniform(arg_keys[6], (2, NLAT, NLON), jnp.float32, -0.48, 0.48) * steps_of(arg_keys[6], (2, NLAT, NLON), ((1, 16), (2, 32)), -0.4, 0.0), -0.48, 0.48),
    }


def upwind(padded, east_west, north_south):
    center = padded[:, 1:-1, 1:-1]
    western = padded[:, 1:-1, :-2]
    eastern = padded[:, 1:-1, 2:]
    southern = padded[:, :-2, 1:-1]
    northern = padded[:, 2:, 1:-1]
    zonal = jnp.maximum(east_west, 0.0) * (center - western) + jnp.minimum(east_west, 0.0) * (eastern - center)
    meridional = jnp.maximum(north_south, 0.0) * (center - southern) + jnp.minimum(north_south, 0.0) * (northern - center)
    return center - zonal - meridional

def advance(current, courant):
    for step_index in range(STEPS):
        padded = jnp.pad(current, ((0, 0), (1, 1), (0, 0)))
        padded = jnp.concatenate([padded[:, :, -1:], padded, padded[:, :, :1]], axis=2)
        current = upwind(padded, courant[0], courant[1])
    return current

def reference(control, perturb, lon_loc, lat_loc, static_scale, static_field, courant):
    members = control.shape[0]
    fields = control.shape[1]
    lon_full = lon_loc.astype(jnp.float32)
    lat_full = lat_loc.astype(jnp.float32)

    def add_member(total, pair):
        control_one, perturb_one = pair
        flat = control_one.astype(jnp.float32).reshape(fields * NLAT, NLON)
        along_lon = jnp.dot(flat, lon_full, precision=lax.Precision.HIGHEST)
        along_lon = along_lon.astype(jnp.bfloat16).astype(jnp.float32).reshape(fields, NLAT, NLON)
        localized = jnp.einsum('ab,fbl->fal', lat_full, along_lon, precision=lax.Precision.HIGHEST)
        return (total + localized * perturb_one.astype(jnp.float32), None)
    total, unused = lax.scan(add_member, jnp.zeros((fields, NLAT, NLON), jnp.float32), (control, perturb))
    ensemble = total * (1.0 / math.sqrt(members - 1))
    increment = ensemble + static_scale * static_field
    evolved = advance(increment, courant)
    return (increment, evolved)
```

```python
import functools
import math

import jax
import jax.numpy as jnp
from jax import lax
from jax.experimental import pallas as pl
from jax.experimental.pallas import tpu as pltpu
from jax.sharding import PartitionSpec as P

STEPS = 4
ZLO = 8
CORES = 2
XY = 16
ZHI = 2
MEM = ZLO * CORES
LAT = XY * ZHI
FIELDS = 10
HALF = FIELDS // 2
LOCAL = 2
NLAT = 704
NLON = 1440
BAND = NLAT // LAT
BAND_PAD = 24
WIDTH = NLON // LAT
ROWS = NLAT // MEM
ROWS_EXT = ROWS + 2 * STEPS
ROWS_PAD = 56
LON_BLOCK = NLON // MEM
LAT_BLOCK = 2 * BAND_PAD
PACKED = LOCAL * HALF * WIDTH
SUMMED = HALF * WIDTH
EXPANDED = MEM * ROWS_PAD
MESH = pl.DeviceIdType.MESH
SCALE = 1.0 / math.sqrt(31.0)
NT = (((1,), (1,)), ((), ()))
NN = (((1,), (0,)), ((), ()))


def matmul(a, b, dims):
    return lax.dot_general(a, b, dims, preferred_element_type=jnp.float32)


def kernel(
    control_hbm, perturb_hbm, lon_hbm, lat_hbm, scale_ref, field_ref, courant_ref,
    inc_out, evo_out,
    control, members, lon_all, lat_all, packed, spread, expand, lat_t, pert_t,
    sum_send, sum_recv, rows_send, rows_recv, static_ext, wind, wind_send, wind_recv,
    state, edge_send, edge_recv,
    local_sem, up_send, up_recv, down_send, down_recv, twin_send, twin_recv,
    mem_send, mem_recv, pack_send, pack_recv, total_send, total_recv,
    rim_send, rim_recv, wind_ssem, wind_rsem, edge_ssem, edge_rsem,
):
    i = lax.axis_index("mem")
    j = lax.axis_index("lat")
    zl, c = i // 2, i % 2
    xy, h = j // 2, j % 2
    twin = 2 * zl + 1 - c
    above = (h * ZLO + zl + 1) % 16
    below = (h * ZLO + zl + 15) % 16

    def at(mem, lat):
        return {"mem": mem, "lat": lat}

    up_dev = at(2 * (above % ZLO) + c, 2 * xy + above // ZLO)
    down_dev = at(2 * (below % ZLO) + c, 2 * xy + below // ZLO)
    twin_dev = at(twin, j)

    def remote(src, dst, ssem, rsem, dev):
        return pltpu.make_async_remote_copy(
            src_ref=src, dst_ref=dst, send_sem=ssem, recv_sem=rsem,
            device_id=dev, device_id_type=MESH,
        )

    get_control = pltpu.make_async_copy(control_hbm, control, local_sem.at[0])
    get_lon = pltpu.make_async_copy(lon_hbm, lon_all.at[i], local_sem.at[1])
    get_lat = pltpu.make_async_copy(lat_hbm, lat_all.at[i], local_sem.at[2])
    get_members = pltpu.make_async_copy(perturb_hbm.at[c], members.at[c], local_sem.at[3])
    get_lon.start()
    get_control.start()
    get_lat.start()
    get_members.start()

    barrier = pltpu.get_barrier_semaphore()

    def greet(mem, lat):
        pl.semaphore_signal(barrier, inc=1, device_id=at(mem, lat), device_id_type=MESH)

    greet(2 * (above % ZLO) + c, 2 * xy + above // ZLO)
    greet(2 * (below % ZLO) + c, 2 * xy + below // ZLO)
    greet(twin, j)

    def greet_lat(k, carry):
        other = (j + k) % LAT
        greet(i, other)
        greet(twin, other)
        return carry

    lax.fori_loop(1, LAT, greet_lat, 0)

    def greet_mem(k, carry):
        other = (zl + k) % ZLO
        greet(2 * other, j)
        greet(2 * other + 1, j)
        return carry

    lax.fori_loop(1, ZLO, greet_mem, 0)
    pl.semaphore_wait(barrier, 3 + 2 * (LAT - 1) + 2 * (ZLO - 1))

    def pair(p, send, recv, slot, dev, first=False):
        lon_src = lon_hbm if first else lon_all.at[p]
        lat_src = lat_hbm if first else lat_all.at[p]
        return (
            remote(lon_src, lon_all.at[p], send.at[0, slot], recv.at[0, slot], dev),
            remote(lat_src, lat_all.at[p], send.at[1, slot], recv.at[1, slot], dev),
        )

    def start(copies):
        for copy in copies:
            copy.start()

    start(pair(i, up_send, up_recv, 0, up_dev, True))
    start(pair(i, down_send, down_recv, 0, down_dev, True))
    start(pair(i, twin_send, twin_recv, zl, twin_dev, True))

    product = scale_ref[...] * field_ref[...]
    static_ext[:, STEPS : STEPS + ROWS, :] = product
    rows_send[0, :FIELDS] = product[:, :8, :]
    rows_send[1, :FIELDS] = product[:, ROWS - 8 :, :]
    rows_send[0, FIELDS:] = courant_ref[:, :8, :]
    rows_send[1, FIELDS:] = courant_ref[:, ROWS - 8 :, :]
    first_row, last_row = i == 0, i == MEM - 1

    @pl.when(first_row)
    def _():
        rows_recv[0] = jnp.zeros(rows_recv.shape[1:], rows_recv.dtype)

    @pl.when(last_row)
    def _():
        rows_recv[1] = jnp.zeros(rows_recv.shape[1:], rows_recv.dtype)

    to_before = remote(rows_send.at[0], rows_recv.at[1], rim_send.at[0], rim_recv.at[1], at(jnp.maximum(i - 1, 0), j))
    to_after = remote(rows_send.at[1], rows_recv.at[0], rim_send.at[1], rim_recv.at[0], at(jnp.minimum(i + 1, MEM - 1), j))
    give_members = remote(
        perturb_hbm.at[1 - c], members.at[c], mem_send.at[0], mem_recv.at[0], twin_dev
    )

    get_lon.wait()
    get_control.wait()

    def relay(d):
        wait_from = pair((2 * ((zl + ZLO - d) % ZLO) + c), up_send, up_recv, d - 1, up_dev)
        for copy in wait_from:
            copy.wait_recv()
        p = 2 * ((zl + ZLO - d) % ZLO) + c
        if d < 4:
            start(pair(p, up_send, up_recv, d, up_dev))
        start(pair(p, twin_send, twin_recv, (zl + ZLO - d) % ZLO, twin_dev))
        if d < 4:
            q = 2 * ((zl + d) % ZLO) + c
            for copy in pair(q, down_send, down_recv, d - 1, down_dev):
                copy.wait_recv()
            if d < 3:
                start(pair(q, down_send, down_recv, d, down_dev))
            start(pair(q, twin_send, twin_recv, (zl + d) % ZLO, twin_dev))

    def block(n, carry):
        d = (n + 2) // 4
        r = (n + 2) % 4
        middle = (d + 3) // 4 - d // 4
        other = middle * (r // 2) + (1 - middle) * (r % 2)
        downward = middle * (r % 2)
        source = (zl + d * (2 * downward - 1) + ZLO) % ZLO
        p = 2 * source + (c + other) % 2

        @pl.when(n == 1)
        def _():
            relay(1)

        @pl.when(n == 4)
        def _():
            relay(2)

        @pl.when(n == 8)
        def _():
            relay(3)

        @pl.when(n == 12)
        def _():
            relay(4)

        @pl.when(other == 1)
        def _():
            for copy in pair(p, twin_send, twin_recv, source, twin_dev):
                copy.wait_recv()

        along = matmul(control[...], lon_all[p], NT)
        for hh in range(ZHI):
            for cc in range(CORES):
                pieces = [
                    along[
                        BAND_PAD * (m * FIELDS + cc * HALF + f) : BAND_PAD * (m * FIELDS + cc * HALF + f + 1),
                        WIDTH * hh : WIDTH * (hh + 1),
                    ]
                    for m in range(LOCAL)
                    for f in range(HALF)
                ]
                packed[p, hh, cc] = jnp.concatenate(pieces, axis=1).astype(jnp.bfloat16)
        for hh in range(ZHI):
            for cc in range(CORES):
                mine = jnp.logical_and(p == xy, jnp.logical_and(h == hh, c == cc))

                @pl.when(mine)
                def _():
                    pltpu.make_async_copy(packed.at[p, hh, cc], spread.at[c, j], pack_recv.at[c, j]).start()

                @pl.when(jnp.logical_not(mine))
                def _():
                    remote(
                        packed.at[p, hh, cc], spread.at[c, j],
                        pack_send.at[p, hh, cc], pack_recv.at[c, j],
                        at(2 * zl + cc, 2 * p + hh),
                    ).start()

        @pl.when(n == 1)
        def _():
            give_members.start()

            @pl.when(jnp.logical_not(first_row))
            def _():
                to_before.start()

            @pl.when(jnp.logical_not(last_row))
            def _():
                to_after.start()

        return carry

    lax.fori_loop(0, MEM, block, 0)

    @pl.when(jnp.logical_not(first_row))
    def _():
        to_after.wait_recv()
        to_before.wait_send()

    @pl.when(jnp.logical_not(last_row))
    def _():
        to_before.wait_recv()
        to_after.wait_send()

    static_ext[:, :STEPS, :] = rows_recv[0, :FIELDS, 8 - STEPS :, :]
    static_ext[:, STEPS + ROWS : ROWS_EXT, :] = rows_recv[1, :FIELDS, :STEPS, :]
    static_ext[:, ROWS_EXT:, :] = jnp.zeros((FIELDS, ROWS_PAD - ROWS_EXT, WIDTH), jnp.float32)
    wind[...] = jnp.zeros_like(wind)
    wind[:, :STEPS, STEPS : STEPS + WIDTH] = rows_recv[0, FIELDS:, 8 - STEPS :, :]
    wind[:, STEPS : STEPS + ROWS, STEPS : STEPS + WIDTH] = courant_ref[...]
    wind[:, STEPS + ROWS : ROWS_EXT, STEPS : STEPS + WIDTH] = rows_recv[1, FIELDS:, :STEPS, :]
    for side, low in enumerate((STEPS, WIDTH)):
        wind_send[side] = jnp.concatenate([wind[k, :, low : low + STEPS] for k in range(2)], axis=1)
    west, east = (j + LAT - 1) % LAT, (j + 1) % LAT
    wind_west = remote(wind_send.at[0], wind_recv.at[1], wind_ssem.at[0], wind_rsem.at[1], at(i, west))
    wind_east = remote(wind_send.at[1], wind_recv.at[0], wind_ssem.at[1], wind_rsem.at[0], at(i, east))
    wind_west.start()
    wind_east.start()

    def select_rows(k, carry):
        row = lax.broadcasted_iota(jnp.int32, (ROWS_PAD, NLAT), 0)
        col = lax.broadcasted_iota(jnp.int32, (ROWS_PAD, NLAT), 1)
        hit = jnp.logical_and(col == row + (ROWS * k - STEPS), row < ROWS_EXT)
        expand[k] = jnp.where(hit, 1.0, 0.0).astype(jnp.bfloat16)
        return carry

    lax.fori_loop(0, MEM, select_rows, 0)
    get_lat.wait()
    lat_flat = lat_all[...].reshape(MEM * LAT_BLOCK, NLAT)
    rows_half = EXPANDED // 2
    for part in range(2):
        chooser = expand[part * ZLO : (part + 1) * ZLO].reshape(rows_half, NLAT)
        lat_t[part] = matmul(chooser, lat_flat, NT).astype(jnp.bfloat16)
    get_members.wait()
    give_members.wait()
    for part in range(2):
        chooser = expand[part * ZLO : (part + 1) * ZLO].reshape(rows_half, NLAT)
        for s in range(CORES):
            pert_t[part, s] = matmul(chooser, members[s], NT).astype(jnp.bfloat16)

    wind_west.wait()
    wind_east.wait()
    for k in range(2):
        wind[k, :, :STEPS] = wind_recv[0, :, STEPS * k : STEPS * (k + 1)]
        wind[k, :, STEPS + WIDTH : 2 * STEPS + WIDTH] = wind_recv[1, :, STEPS * k : STEPS * (k + 1)]

    def arrived(k, carry):
        for s in range(CORES):
            remote(packed.at[0, 0, 0], spread.at[s, k], pack_send.at[0, 0, 0], pack_recv.at[s, k], twin_dev).wait_recv()
        return carry

    lax.fori_loop(0, LAT, arrived, 0)
    for part in range(2):
        total = None
        for s in range(CORES):
            term = matmul(lat_t[part], spread[s].reshape(LAT * BAND_PAD, PACKED), NN)
            term = term * pert_t[part, s].astype(jnp.float32)
            total = term if total is None else total + term
        summed = (total[:, :SUMMED] + total[:, SUMMED:]) * SCALE
        sum_send[part * ZLO : (part + 1) * ZLO] = summed.astype(jnp.bfloat16).reshape(ZLO, ROWS_PAD, SUMMED)

        def give(k, carry):
            owner = part * ZLO + k

            @pl.when(owner == i)
            def _():
                pltpu.make_async_copy(sum_send.at[owner], sum_recv.at[i], total_recv.at[i]).start()

            @pl.when(owner != i)
            def _():
                remote(sum_send.at[owner], sum_recv.at[i], total_send.at[owner], total_recv.at[i], at(owner, j)).start()

            return carry

        lax.fori_loop(0, ZLO, give, 0)

    def gathered(k, carry):
        remote(sum_send.at[0], sum_recv.at[k], total_send.at[0], total_recv.at[k], twin_dev).wait_recv()
        return carry

    lax.fori_loop(0, MEM, gathered, 0)
    state[...] = jnp.zeros_like(state)
    for s in range(CORES):
        ensemble = sum_recv[s].astype(jnp.float32)
        for z in range(1, ZLO):
            ensemble = ensemble + sum_recv[CORES * z + s].astype(jnp.float32)
        for f in range(HALF):
            field = ensemble[:, WIDTH * f : WIDTH * (f + 1)] + static_ext[s * HALF + f]
            state[s * HALF + f, :, STEPS : STEPS + WIDTH] = field
            inc_out[s * HALF + f] = field[STEPS : STEPS + ROWS, :]
    for side, low in enumerate((STEPS, WIDTH)):
        edge_send[side] = jnp.concatenate([state[f, :, low : low + STEPS] for f in range(FIELDS)], axis=1)
    edge_west = remote(edge_send.at[0], edge_recv.at[1], edge_ssem.at[0], edge_rsem.at[1], at(i, west))
    edge_east = remote(edge_send.at[1], edge_recv.at[0], edge_ssem.at[1], edge_rsem.at[0], at(i, east))
    edge_west.start()
    edge_east.start()

    for slot in range(4):
        for copy in pair(0, up_send, up_recv, slot, up_dev):
            copy.wait_send()
    for slot in range(3):
        for copy in pair(0, down_send, down_recv, slot, down_dev):
            copy.wait_send()

    def twins(k, carry):
        for copy in pair(0, twin_send, twin_recv, k, twin_dev):
            copy.wait_send()
        return carry

    lax.fori_loop(0, ZLO, twins, 0)

    def packs(p, carry):
        for hh in range(ZHI):
            for cc in range(CORES):
                mine = jnp.logical_and(p == xy, jnp.logical_and(h == hh, c == cc))

                @pl.when(jnp.logical_not(mine))
                def _():
                    remote(
                        packed.at[p, hh, cc], spread.at[0, 0], pack_send.at[p, hh, cc], pack_recv.at[0, 0], twin_dev
                    ).wait_send()

        return carry

    lax.fori_loop(0, MEM, packs, 0)

    def totals(k, carry):
        @pl.when(k != i)
        def _():
            remote(sum_send.at[k], sum_recv.at[0], total_send.at[k], total_recv.at[0], twin_dev).wait_send()

        return carry

    lax.fori_loop(0, MEM, totals, 0)

    edge_west.wait()
    edge_east.wait()
    u, v = wind[0], wind[1]
    u_pos, u_neg = jnp.maximum(u, 0.0), jnp.minimum(u, 0.0)
    v_pos, v_neg = jnp.maximum(v, 0.0), jnp.minimum(v, 0.0)
    for f in range(FIELDS):
        state[f, :, :STEPS] = edge_recv[0, :, STEPS * f : STEPS * (f + 1)]
        state[f, :, STEPS + WIDTH : 2 * STEPS + WIDTH] = edge_recv[1, :, STEPS * f : STEPS * (f + 1)]

    def advance(f, carry):
        q = state[f]
        for _ in range(STEPS):
            western = pltpu.roll(q, 1, 1)
            eastern = pltpu.roll(q, q.shape[1] - 1, 1)
            southern = pltpu.roll(q, 1, 0)
            northern = pltpu.roll(q, q.shape[0] - 1, 0)
            zonal = u_pos * (q - western) + u_neg * (eastern - q)
            meridional = v_pos * (q - southern) + v_neg * (northern - q)
            q = q - zonal - meridional
        evo_out[f] = q[STEPS : STEPS + ROWS, STEPS : STEPS + WIDTH]
        return carry

    lax.fori_loop(0, FIELDS, advance, 0)


def per_device(control, perturb, lon_loc, lat_loc, static_scale, static_field, courant):
    rows = jnp.pad(control, ((0, 0), (0, 0), (0, BAND_PAD - BAND), (0, 0)))
    rows = rows.reshape(LOCAL * FIELDS * BAND_PAD, NLON)
    halves = perturb.reshape(LOCAL, CORES, HALF, NLAT, WIDTH).transpose(1, 0, 2, 4, 3)
    halves = halves.reshape(CORES, PACKED, NLAT)
    lat_rows = jnp.pad(lat_loc.reshape(2, BAND, NLAT), ((0, 0), (0, BAND_PAD - BAND), (0, 0)))
    lat_rows = lat_rows.reshape(LAT_BLOCK, NLAT)
    anywhere = pl.BlockSpec(memory_space=pl.ANY)
    vmem = pl.BlockSpec(memory_space=pltpu.VMEM)
    bf16, f32 = jnp.bfloat16, jnp.float32
    dma = pltpu.SemaphoreType.DMA
    out = jax.ShapeDtypeStruct((FIELDS, ROWS, WIDTH), f32)
    return pl.pallas_call(
        kernel,
        out_shape=(out, out),
        in_specs=[anywhere] * 4 + [vmem] * 3,
        out_specs=(vmem, vmem),
        scratch_shapes=[
            pltpu.VMEM((LOCAL * FIELDS * BAND_PAD, NLON), bf16),
            pltpu.VMEM((CORES, PACKED, NLAT), bf16),
            pltpu.VMEM((MEM, LON_BLOCK, NLON), bf16),
            pltpu.VMEM((MEM, LAT_BLOCK, NLAT), bf16),
            pltpu.VMEM((XY, ZHI, CORES, BAND_PAD, PACKED), bf16),
            pltpu.VMEM((CORES, LAT, BAND_PAD, PACKED), bf16),
            pltpu.VMEM((MEM, ROWS_PAD, NLAT), bf16),
            pltpu.VMEM((2, EXPANDED // 2, LAT * BAND_PAD), bf16),
            pltpu.VMEM((2, CORES, EXPANDED // 2, PACKED), bf16),
            pltpu.VMEM((MEM, ROWS_PAD, SUMMED), bf16),
            pltpu.VMEM((MEM, ROWS_PAD, SUMMED), bf16),
            pltpu.VMEM((2, FIELDS + 2, 8, WIDTH), f32),
            pltpu.VMEM((2, FIELDS + 2, 8, WIDTH), f32),
            pltpu.VMEM((FIELDS, ROWS_PAD, WIDTH), f32),
            pltpu.VMEM((2, ROWS_PAD, 128), f32),
            pltpu.VMEM((2, ROWS_PAD, 2 * STEPS), f32),
            pltpu.VMEM((2, ROWS_PAD, 2 * STEPS), f32),
            pltpu.VMEM((FIELDS, ROWS_PAD, 128), f32),
            pltpu.VMEM((2, ROWS_PAD, FIELDS * STEPS), f32),
            pltpu.VMEM((2, ROWS_PAD, FIELDS * STEPS), f32),
            dma((4,)), dma((2, 4)), dma((2, 4)), dma((2, 3)), dma((2, 3)), dma((2, ZLO)), dma((2, ZLO)),
            dma((1,)), dma((1,)), dma((XY, ZHI, CORES)), dma((CORES, LAT)), dma((MEM,)), dma((MEM,)),
            dma((2,)), dma((2,)), dma((2,)), dma((2,)), dma((2,)), dma((2,)),
        ],
        compiler_params=pltpu.CompilerParams(
            collective_id=0, has_side_effects=True, vmem_limit_bytes=56 * 1024 * 1024
        ),
        name="increment",
    )(rows, halves, lon_loc.T, lat_rows, static_scale, static_field, courant)


def solution(mesh):
    placed = (
        P("mem", None, "lat", None),
        P("mem", None, None, "lat"),
        P(None, "mem"),
        P("mem", None),
        P(None, "mem", "lat"),
        P(None, "mem", "lat"),
        P(None, "mem", "lat"),
    )
    return jax.shard_map(
        per_device,
        mesh=mesh,
        in_specs=placed,
        out_specs=(P(None, "mem", "lat"), P(None, "mem", "lat")),
        check_vma=False,
    )
```

```python
import functools
import math

import jax
import jax.numpy as jnp
from jax import lax
from jax.experimental import pallas as pl
from jax.experimental.pallas import tpu as pltpu
from jax.sharding import PartitionSpec as P

STEPS = 4
ZLO = 8
CORES = 2
XY = 16
ZHI = 2
MEM = ZLO * CORES
LAT = XY * ZHI
FIELDS = 10
HALF = FIELDS // 2
LOCAL = 2
NLAT = 704
NLON = 1440
BAND = NLAT // LAT
BAND_PAD = 24
WIDTH = NLON // LAT
ROWS = NLAT // MEM
ROWS_EXT = ROWS + 2 * STEPS
ROWS_PAD = 56
LON_BLOCK = NLON // MEM
LAT_BLOCK = 2 * BAND_PAD
QUARTERS = 4
LANES = 128
WHOLE = 3 * LANES
REST = LOCAL * HALF * WIDTH - WHOLE
FOLD = LANES - REST
WIRE_ROWS = 3 * BAND_PAD + 16
PACKED = LOCAL * HALF * WIDTH
SUMMED = HALF * WIDTH
EXPANDED = MEM * ROWS_PAD
MESH = pl.DeviceIdType.MESH
SCALE = 1.0 / math.sqrt(31.0)
NT = (((1,), (1,)), ((), ()))
NN = (((1,), (0,)), ((), ()))


def matmul(a, b, dims):
    return lax.dot_general(a, b, dims, preferred_element_type=jnp.float32)


def kernel(
    control_hbm, perturb_hbm, lon_hbm, lat_hbm, scale_ref, field_ref, courant_ref,
    inc_out, evo_out,
    control, members, lon_all, lat_all, packed, spread, expand, lat_t, pert_t,
    rest, sum_send, sum_recv, rows_send, rows_recv, static_ext, wind, wind_send, wind_recv,
    state, edge_send, edge_recv,
    local_sem, up_send, up_recv, down_send, down_recv, side_send, side_recv, twin_send, twin_recv,
    mem_send, mem_recv, pack_send, pack_recv, total_send, total_recv,
    rim_send, rim_recv, wind_ssem, wind_rsem, edge_ssem, edge_rsem,
):
    i = lax.axis_index("mem")
    j = lax.axis_index("lat")
    zl, c = i // 2, i % 2
    xy, h = j // 2, j % 2
    x, y = xy // 4, xy % 4
    half = (x + y) % 2
    twin = 2 * zl + 1 - c
    above = (h * ZLO + zl + 1) % 16
    below = (h * ZLO + zl + 15) % 16

    def at(mem, lat):
        return {"mem": mem, "lat": lat}

    up_dev = at(2 * (above % ZLO) + c, 2 * xy + above // ZLO)
    down_dev = at(2 * (below % ZLO) + c, 2 * xy + below // ZLO)
    twin_dev = at(twin, j)
    plus_dev = at(i, 2 * (4 * ((x + 1 - c) % 4) + (y + c) % 4) + h)
    minus_dev = at(i, 2 * (4 * ((x + 3 * (1 - c)) % 4) + (y + 3 * c) % 4) + h)

    def remote(src, dst, ssem, rsem, dev):
        return pltpu.make_async_remote_copy(
            src_ref=src, dst_ref=dst, send_sem=ssem, recv_sem=rsem,
            device_id=dev, device_id_type=MESH,
        )

    get_control = pltpu.make_async_copy(control_hbm, control, local_sem.at[0])
    get_lon = pltpu.make_async_copy(lon_hbm, lon_all.at[i], local_sem.at[1])
    get_lat = pltpu.make_async_copy(lat_hbm, lat_all.at[i], local_sem.at[2])
    get_members = pltpu.make_async_copy(perturb_hbm.at[c], members.at[c], local_sem.at[3])
    get_lon.start()
    get_control.start()
    get_lat.start()
    get_members.start()

    barrier = pltpu.get_barrier_semaphore()

    def greet(mem, lat):
        pl.semaphore_signal(barrier, inc=1, device_id=at(mem, lat), device_id_type=MESH)

    greet(2 * (above % ZLO) + c, 2 * xy + above // ZLO)
    greet(2 * (below % ZLO) + c, 2 * xy + below // ZLO)
    greet(twin, j)

    def greet_lat(k, carry):
        other = (j + k) % LAT
        greet(i, other)
        greet(twin, other)
        return carry

    lax.fori_loop(1, LAT, greet_lat, 0)

    def greet_mem(k, carry):
        other = (zl + k) % ZLO
        greet(2 * other, j)
        greet(2 * other + 1, j)
        return carry

    lax.fori_loop(1, ZLO, greet_mem, 0)
    pl.semaphore_wait(barrier, 3 + 2 * (LAT - 1) + 2 * (ZLO - 1))

    get_lon.wait()
    get_lat.wait()

    def ring(p, send, recv, slot, dev):
        part = lon_all.at[p, pl.ds(2 * half, 2)]
        return (
            remote(part, part, send.at[0, slot], recv.at[0, slot], dev),
            remote(lat_all.at[p, half], lat_all.at[p, half], send.at[1, slot], recv.at[1, slot], dev),
        )

    def beside(p, mine, slot):
        first, second = lon_all.at[p, 2 * mine], lon_all.at[p, 2 * mine + 1]
        third = lat_all.at[p, mine]
        return (
            remote(first, first, side_send.at[0, slot], side_recv.at[0, slot], plus_dev),
            remote(second, second, side_send.at[1, slot], side_recv.at[1, slot], minus_dev),
            remote(third, third, side_send.at[2, slot], side_recv.at[2, slot], plus_dev),
        )

    def across(p, slot):
        return (
            remote(lon_all.at[p], lon_all.at[p], twin_send.at[0, slot], twin_recv.at[0, slot], twin_dev),
            remote(lat_all.at[p], lat_all.at[p], twin_send.at[1, slot], twin_recv.at[1, slot], twin_dev),
        )

    def start(copies):
        for copy in copies:
            copy.start()

    start(ring(i, up_send, up_recv, 0, up_dev))
    start(ring(i, down_send, down_recv, 0, down_dev))
    start(across(i, zl))

    product = scale_ref[...] * field_ref[...]
    static_ext[:, STEPS : STEPS + ROWS, :] = product
    rows_send[0, :FIELDS] = product[:, :8, :]
    rows_send[1, :FIELDS] = product[:, ROWS - 8 :, :]
    rows_send[0, FIELDS:] = courant_ref[:, :8, :]
    rows_send[1, FIELDS:] = courant_ref[:, ROWS - 8 :, :]
    first_row, last_row = i == 0, i == MEM - 1

    @pl.when(first_row)
    def _():
        rows_recv[0] = jnp.zeros(rows_recv.shape[1:], rows_recv.dtype)

    @pl.when(last_row)
    def _():
        rows_recv[1] = jnp.zeros(rows_recv.shape[1:], rows_recv.dtype)

    to_before = remote(rows_send.at[0], rows_recv.at[1], rim_send.at[0], rim_recv.at[1], at(jnp.maximum(i - 1, 0), j))
    to_after = remote(rows_send.at[1], rows_recv.at[0], rim_send.at[1], rim_recv.at[0], at(jnp.minimum(i + 1, MEM - 1), j))
    give_members = remote(
        perturb_hbm.at[1 - c], members.at[c], mem_send.at[0], mem_recv.at[0], twin_dev
    )

    get_control.wait()

    def relay(d):
        source = (zl + ZLO - d) % ZLO
        for copy in ring(2 * source + c, up_send, up_recv, d - 1, up_dev):
            copy.wait_recv()
        if d < 4:
            start(ring(2 * source + c, up_send, up_recv, d, up_dev))
        start(beside(2 * source + c, half, source))
        if d < 4:
            source = (zl + d) % ZLO
            for copy in ring(2 * source + c, down_send, down_recv, d - 1, down_dev):
                copy.wait_recv()
            if d < 3:
                start(ring(2 * source + c, down_send, down_recv, d, down_dev))
            start(beside(2 * source + c, half, source))

    def complete(d):
        for step in (-1, 1) if d < 4 else (-1,):
            source = (zl + ZLO + step * d) % ZLO
            for copy in beside(2 * source + c, 1 - half, source):
                copy.wait_recv()
            start(across(2 * source + c, source))

    def block(n, carry):
        d = (n + 2) // 4
        r = (n + 2) % 4
        middle = (d + 3) // 4 - d // 4
        other = middle * (r // 2) + (1 - middle) * (r % 2)
        downward = middle * (r % 2)
        source = (zl + d * (2 * downward - 1) + ZLO) % ZLO
        p = 2 * source + (c + other) % 2

        for d in range(1, 5):

            @pl.when(n == (1 if d == 1 else 4 * (d - 1)))
            def _():
                relay(d)

            @pl.when(n == 4 * d - 2)
            def _():
                complete(d)

        @pl.when(other == 1)
        def _():
            for copy in across(p, source):
                copy.wait_recv()

        lon_rows = lon_all[p].reshape(QUARTERS * BAND_PAD, NLON)
        along = matmul(control[...], lon_rows, NT)
        lane = lax.broadcasted_iota(jnp.int32, (8, LANES), 1)
        for hh in range(ZHI):
            for cc in range(CORES):
                pieces = [
                    along[
                        BAND_PAD * (m * FIELDS + cc * HALF + f) : BAND_PAD * (m * FIELDS + cc * HALF + f + 1),
                        WIDTH * hh : WIDTH * (hh + 1),
                    ]
                    for m in range(LOCAL)
                    for f in range(HALF)
                ]
                pieces.append(jnp.zeros((BAND_PAD, FOLD), jnp.float32))
                row = jnp.concatenate(pieces, axis=1)
                last = row[:, WHOLE:]
                low, middle_rows, high = last[:8], last[8:16], last[16:]
                folded = jnp.concatenate(
                    [
                        jnp.where(lane < REST, low, pltpu.roll(high, REST, 1)),
                        jnp.where(
                            lane < REST,
                            middle_rows,
                            jnp.where(lane < 2 * REST - FOLD, pltpu.roll(high, REST - FOLD, 1), 0.0),
                        ),
                    ],
                    axis=0,
                )
                wire = [row[:, LANES * t : LANES * (t + 1)] for t in range(3)] + [folded]
                packed[p, hh, cc] = jnp.concatenate(wire, axis=0).astype(jnp.bfloat16)
        for hh in range(ZHI):
            for cc in range(CORES):
                mine = jnp.logical_and(p == xy, jnp.logical_and(h == hh, c == cc))

                @pl.when(mine)
                def _():
                    pltpu.make_async_copy(packed.at[p, hh, cc], spread.at[c, j], pack_recv.at[c, j]).start()

                @pl.when(jnp.logical_not(mine))
                def _():
                    remote(
                        packed.at[p, hh, cc], spread.at[c, j],
                        pack_send.at[p, hh, cc], pack_recv.at[c, j],
                        at(2 * zl + cc, 2 * p + hh),
                    ).start()

        @pl.when(n == 1)
        def _():
            give_members.start()

            @pl.when(jnp.logical_not(first_row))
            def _():
                to_before.start()

            @pl.when(jnp.logical_not(last_row))
            def _():
                to_after.start()

        return carry

    lax.fori_loop(0, MEM, block, 0)

    @pl.when(jnp.logical_not(first_row))
    def _():
        to_after.wait_recv()
        to_before.wait_send()

    @pl.when(jnp.logical_not(last_row))
    def _():
        to_before.wait_recv()
        to_after.wait_send()

    static_ext[:, :STEPS, :] = rows_recv[0, :FIELDS, 8 - STEPS :, :]
    static_ext[:, STEPS + ROWS : ROWS_EXT, :] = rows_recv[1, :FIELDS, :STEPS, :]
    static_ext[:, ROWS_EXT:, :] = jnp.zeros((FIELDS, ROWS_PAD - ROWS_EXT, WIDTH), jnp.float32)
    wind[...] = jnp.zeros_like(wind)
    wind[:, :STEPS, STEPS : STEPS + WIDTH] = rows_recv[0, FIELDS:, 8 - STEPS :, :]
    wind[:, STEPS : STEPS + ROWS, STEPS : STEPS + WIDTH] = courant_ref[...]
    wind[:, STEPS + ROWS : ROWS_EXT, STEPS : STEPS + WIDTH] = rows_recv[1, FIELDS:, :STEPS, :]
    for side, low in enumerate((STEPS, WIDTH)):
        wind_send[side] = jnp.concatenate([wind[k, :, low : low + STEPS] for k in range(2)], axis=1)
    west, east = (j + LAT - 1) % LAT, (j + 1) % LAT
    wind_west = remote(wind_send.at[0], wind_recv.at[1], wind_ssem.at[0], wind_rsem.at[1], at(i, west))
    wind_east = remote(wind_send.at[1], wind_recv.at[0], wind_ssem.at[1], wind_rsem.at[0], at(i, east))
    wind_west.start()
    wind_east.start()

    def select_rows(k, carry):
        row = lax.broadcasted_iota(jnp.int32, (ROWS_PAD, NLAT), 0)
        col = lax.broadcasted_iota(jnp.int32, (ROWS_PAD, NLAT), 1)
        hit = jnp.logical_and(col == row + (ROWS * k - STEPS), row < ROWS_EXT)
        expand[k] = jnp.where(hit, 1.0, 0.0).astype(jnp.bfloat16)
        return carry

    lax.fori_loop(0, MEM, select_rows, 0)
    lat_flat = lat_all[...].reshape(MEM * LAT_BLOCK, NLAT)
    rows_half = EXPANDED // 2
    for part in range(2):
        chooser = expand[part * ZLO : (part + 1) * ZLO].reshape(rows_half, NLAT)
        lat_t[part] = matmul(chooser, lat_flat, NT).astype(jnp.bfloat16)
    get_members.wait()
    give_members.wait()
    for part in range(2):
        chooser = expand[part * ZLO : (part + 1) * ZLO].reshape(rows_half, NLAT)
        for s in range(CORES):
            pert_t[part, s] = matmul(chooser, members[s], NT).astype(jnp.bfloat16)

    wind_west.wait()
    wind_east.wait()
    for k in range(2):
        wind[k, :, :STEPS] = wind_recv[0, :, STEPS * k : STEPS * (k + 1)]
        wind[k, :, STEPS + WIDTH : 2 * STEPS + WIDTH] = wind_recv[1, :, STEPS * k : STEPS * (k + 1)]

    lane = lax.broadcasted_iota(jnp.int32, (8, LANES), 1)

    def arrived(k, carry):
        for s in range(CORES):
            remote(packed.at[0, 0, 0], spread.at[s, k], pack_send.at[0, 0, 0], pack_recv.at[s, k], twin_dev).wait_recv()
            folded = spread[s, k, 3 * BAND_PAD :, :].astype(jnp.float32)
            low, middle_rows = folded[:8], folded[8:]
            high = jnp.where(
                lane < FOLD, pltpu.roll(low, FOLD, 1), pltpu.roll(middle_rows, LANES - REST + FOLD, 1)
            )
            rest[s, k] = jnp.concatenate([low, middle_rows, high], axis=0).astype(jnp.bfloat16)
        return carry

    lax.fori_loop(0, LAT, arrived, 0)
    for part in range(2):
        total = None
        for s in range(CORES):
            tiles = [spread[s, :, BAND_PAD * t : BAND_PAD * (t + 1), :] for t in range(3)] + [rest[s]]
            tiles = [t.reshape(LAT * BAND_PAD, LANES) for t in tiles]
            term = matmul(lat_t[part], jnp.concatenate(tiles, axis=1), NN)[:, :PACKED]
            term = term * pert_t[part, s].astype(jnp.float32)
            total = term if total is None else total + term
        summed = (total[:, :SUMMED] + total[:, SUMMED:]) * SCALE
        sum_send[part * ZLO : (part + 1) * ZLO] = summed.astype(jnp.bfloat16).reshape(ZLO, ROWS_PAD, SUMMED)

        def give(k, carry):
            owner = part * ZLO + k

            @pl.when(owner == i)
            def _():
                pltpu.make_async_copy(sum_send.at[owner], sum_recv.at[i], total_recv.at[i]).start()

            @pl.when(owner != i)
            def _():
                remote(sum_send.at[owner], sum_recv.at[i], total_send.at[owner], total_recv.at[i], at(owner, j)).start()

            return carry

        lax.fori_loop(0, ZLO, give, 0)

    def gathered(k, carry):
        remote(sum_send.at[0], sum_recv.at[k], total_send.at[0], total_recv.at[k], twin_dev).wait_recv()
        return carry

    lax.fori_loop(0, MEM, gathered, 0)
    state[...] = jnp.zeros_like(state)
    for s in range(CORES):
        ensemble = sum_recv[s].astype(jnp.float32)
        for z in range(1, ZLO):
            ensemble = ensemble + sum_recv[CORES * z + s].astype(jnp.float32)
        for f in range(HALF):
            field = ensemble[:, WIDTH * f : WIDTH * (f + 1)] + static_ext[s * HALF + f]
            state[s * HALF + f, :, STEPS : STEPS + WIDTH] = field
            inc_out[s * HALF + f] = field[STEPS : STEPS + ROWS, :]
    for side, low in enumerate((STEPS, WIDTH)):
        edge_send[side] = jnp.concatenate([state[f, :, low : low + STEPS] for f in range(FIELDS)], axis=1)
    edge_west = remote(edge_send.at[0], edge_recv.at[1], edge_ssem.at[0], edge_rsem.at[1], at(i, west))
    edge_east = remote(edge_send.at[1], edge_recv.at[0], edge_ssem.at[1], edge_rsem.at[0], at(i, east))
    edge_west.start()
    edge_east.start()

    for slot in range(4):
        for copy in ring(0, up_send, up_recv, slot, up_dev):
            copy.wait_send()
    for slot in range(3):
        for copy in ring(0, down_send, down_recv, slot, down_dev):
            copy.wait_send()

    def twins(k, carry):
        for copy in across(0, k):
            copy.wait_send()

        @pl.when(k != zl)
        def _():
            for copy in beside(0, half, k):
                copy.wait_send()

        return carry

    lax.fori_loop(0, ZLO, twins, 0)

    def packs(p, carry):
        for hh in range(ZHI):
            for cc in range(CORES):
                mine = jnp.logical_and(p == xy, jnp.logical_and(h == hh, c == cc))

                @pl.when(jnp.logical_not(mine))
                def _():
                    remote(
                        packed.at[p, hh, cc], spread.at[0, 0], pack_send.at[p, hh, cc], pack_recv.at[0, 0], twin_dev
                    ).wait_send()

        return carry

    lax.fori_loop(0, MEM, packs, 0)

    def totals(k, carry):
        @pl.when(k != i)
        def _():
            remote(sum_send.at[k], sum_recv.at[0], total_send.at[k], total_recv.at[0], twin_dev).wait_send()

        return carry

    lax.fori_loop(0, MEM, totals, 0)

    edge_west.wait()
    edge_east.wait()
    u, v = wind[0], wind[1]
    u_pos, u_neg = jnp.maximum(u, 0.0), jnp.minimum(u, 0.0)
    v_pos, v_neg = jnp.maximum(v, 0.0), jnp.minimum(v, 0.0)
    for f in range(FIELDS):
        state[f, :, :STEPS] = edge_recv[0, :, STEPS * f : STEPS * (f + 1)]
        state[f, :, STEPS + WIDTH : 2 * STEPS + WIDTH] = edge_recv[1, :, STEPS * f : STEPS * (f + 1)]

    def advance(f, carry):
        q = state[f]
        for _ in range(STEPS):
            western = pltpu.roll(q, 1, 1)
            eastern = pltpu.roll(q, q.shape[1] - 1, 1)
            southern = pltpu.roll(q, 1, 0)
            northern = pltpu.roll(q, q.shape[0] - 1, 0)
            zonal = u_pos * (q - western) + u_neg * (eastern - q)
            meridional = v_pos * (q - southern) + v_neg * (northern - q)
            q = q - zonal - meridional
        evo_out[f] = q[STEPS : STEPS + ROWS, STEPS : STEPS + WIDTH]
        return carry

    lax.fori_loop(0, FIELDS, advance, 0)


def per_device(control, perturb, lon_loc, lat_loc, static_scale, static_field, courant):
    rows = jnp.pad(control, ((0, 0), (0, 0), (0, BAND_PAD - BAND), (0, 0)))
    rows = rows.reshape(LOCAL * FIELDS * BAND_PAD, NLON)
    halves = perturb.reshape(LOCAL, CORES, HALF, NLAT, WIDTH).transpose(1, 0, 2, 4, 3)
    halves = halves.reshape(CORES, PACKED, NLAT)
    lat_rows = jnp.pad(lat_loc.reshape(2, BAND, NLAT), ((0, 0), (0, BAND_PAD - BAND), (0, 0)))
    lon_rows = jnp.pad(lon_loc.T, ((0, QUARTERS * BAND_PAD - LON_BLOCK), (0, 0)))
    lon_rows = lon_rows.reshape(QUARTERS, BAND_PAD, NLON)
    anywhere = pl.BlockSpec(memory_space=pl.ANY)
    vmem = pl.BlockSpec(memory_space=pltpu.VMEM)
    bf16, f32 = jnp.bfloat16, jnp.float32
    dma = pltpu.SemaphoreType.DMA
    out = jax.ShapeDtypeStruct((FIELDS, ROWS, WIDTH), f32)
    return pl.pallas_call(
        kernel,
        out_shape=(out, out),
        in_specs=[anywhere] * 4 + [vmem] * 3,
        out_specs=(vmem, vmem),
        scratch_shapes=[
            pltpu.VMEM((LOCAL * FIELDS * BAND_PAD, NLON), bf16),
            pltpu.VMEM((CORES, PACKED, NLAT), bf16),
            pltpu.VMEM((MEM, QUARTERS, BAND_PAD, NLON), bf16),
            pltpu.VMEM((MEM, 2, BAND_PAD, NLAT), bf16),
            pltpu.VMEM((XY, ZHI, CORES, WIRE_ROWS, LANES), bf16),
            pltpu.VMEM((CORES, LAT, WIRE_ROWS, LANES), bf16),
            pltpu.VMEM((MEM, ROWS_PAD, NLAT), bf16),
            pltpu.VMEM((2, EXPANDED // 2, LAT * BAND_PAD), bf16),
            pltpu.VMEM((2, CORES, EXPANDED // 2, PACKED), bf16),
            pltpu.VMEM((CORES, LAT, BAND_PAD, LANES), bf16),
            pltpu.VMEM((MEM, ROWS_PAD, SUMMED), bf16),
            pltpu.VMEM((MEM, ROWS_PAD, SUMMED), bf16),
            pltpu.VMEM((2, FIELDS + 2, 8, WIDTH), f32),
            pltpu.VMEM((2, FIELDS + 2, 8, WIDTH), f32),
            pltpu.VMEM((FIELDS, ROWS_PAD, WIDTH), f32),
            pltpu.VMEM((2, ROWS_PAD, 128), f32),
            pltpu.VMEM((2, ROWS_PAD, 2 * STEPS), f32),
            pltpu.VMEM((2, ROWS_PAD, 2 * STEPS), f32),
            pltpu.VMEM((FIELDS, ROWS_PAD, 128), f32),
            pltpu.VMEM((2, ROWS_PAD, FIELDS * STEPS), f32),
            pltpu.VMEM((2, ROWS_PAD, FIELDS * STEPS), f32),
            dma((4,)), dma((2, 4)), dma((2, 4)), dma((2, 3)), dma((2, 3)), dma((3, ZLO)), dma((3, ZLO)),
            dma((2, ZLO)), dma((2, ZLO)),
            dma((1,)), dma((1,)), dma((XY, ZHI, CORES)), dma((CORES, LAT)), dma((MEM,)), dma((MEM,)),
            dma((2,)), dma((2,)), dma((2,)), dma((2,)), dma((2,)), dma((2,)),
        ],
        compiler_params=pltpu.CompilerParams(
            collective_id=0, has_side_effects=True, vmem_limit_bytes=56 * 1024 * 1024
        ),
        name="increment",
    )(rows, halves, lon_rows, lat_rows, static_scale, static_field, courant)


def solution(mesh):
    placed = (
        P("mem", None, "lat", None),
        P("mem", None, None, "lat"),
        P(None, "mem"),
        P("mem", None),
        P(None, "mem", "lat"),
        P(None, "mem", "lat"),
        P(None, "mem", "lat"),
    )
    return jax.shard_map(
        per_device,
        mesh=mesh,
        in_specs=placed,
        out_specs=(P(None, "mem", "lat"), P(None, "mem", "lat")),
        check_vma=False,
    )
```

```python
import functools
import math

import jax
import jax.numpy as jnp
from jax import lax
from jax.experimental import pallas as pl
from jax.experimental.pallas import tpu as pltpu
from jax.sharding import PartitionSpec as P

STEPS = 4
ZLO = 8
CORES = 2
XY = 16
ZHI = 2
MEM = ZLO * CORES
LAT = XY * ZHI
FIELDS = 10
HALF = FIELDS // 2
LOCAL = 2
NLAT = 704
NLON = 1440
BAND = NLAT // LAT
BAND_PAD = 24
WIDTH = NLON // LAT
ROWS = NLAT // MEM
ROWS_EXT = ROWS + 2 * STEPS
ROWS_PAD = 56
LON_BLOCK = NLON // MEM
LAT_BLOCK = 2 * BAND_PAD
QUARTERS = 4
LANES = 128
WHOLE = 3 * LANES
REST = LOCAL * HALF * WIDTH - WHOLE
FOLD = LANES - REST
WIRE_ROWS = 3 * BAND_PAD + 8
SPARE = REST - FOLD
PACKED = LOCAL * HALF * WIDTH
SUMMED = HALF * WIDTH
EXPANDED = MEM * ROWS_PAD
MESH = pl.DeviceIdType.MESH
SCALE = 1.0 / math.sqrt(31.0)
NT = (((1,), (1,)), ((), ()))
NN = (((1,), (0,)), ((), ()))


def matmul(a, b, dims):
    return lax.dot_general(a, b, dims, preferred_element_type=jnp.float32)


def kernel(
    control_hbm, perturb_hbm, lon_ref, lat_ref, scale_ref, field_ref, courant_ref,
    inc_out, evo_out,
    control_raw, control, members_raw, members, gift, lon_all, lat_all, packed, spread, expand, lat_t, pert_t,
    rest, sum_send, sum_recv, rows_send, rows_recv, static_ext, wind, wind_send, wind_recv,
    state, edge_send, edge_recv,
    local_sem, up_send, up_recv, down_send, down_recv, side_send, side_recv, twin_send, twin_recv,
    mem_send, mem_recv, pack_send, pack_recv, total_send, total_recv,
    rim_send, rim_recv, wind_ssem, wind_rsem, edge_ssem, edge_rsem,
):
    i = lax.axis_index("mem")
    j = lax.axis_index("lat")
    zl, c = i // 2, i % 2
    xy, h = j // 2, j % 2
    x, y = xy // 4, xy % 4
    half = (x + y) % 2
    twin = 2 * zl + 1 - c
    above = (h * ZLO + zl + 1) % 16
    below = (h * ZLO + zl + 15) % 16

    def at(mem, lat):
        return {"mem": mem, "lat": lat}

    up_dev = at(2 * (above % ZLO) + c, 2 * xy + above // ZLO)
    down_dev = at(2 * (below % ZLO) + c, 2 * xy + below // ZLO)
    twin_dev = at(twin, j)
    plus_dev = at(i, 2 * (4 * ((x + 1 - c) % 4) + (y + c) % 4) + h)
    minus_dev = at(i, 2 * (4 * ((x + 3 * (1 - c)) % 4) + (y + 3 * c) % 4) + h)

    def remote(src, dst, ssem, rsem, dev):
        return pltpu.make_async_remote_copy(
            src_ref=src, dst_ref=dst, send_sem=ssem, recv_sem=rsem,
            device_id=dev, device_id_type=MESH,
        )

    get_control = pltpu.make_async_copy(control_hbm, control_raw, local_sem.at[0])
    get_members = pltpu.make_async_copy(perturb_hbm, members_raw, local_sem.at[1])
    get_control.start()
    get_members.start()

    barrier = pltpu.get_barrier_semaphore()

    def greet(mem, lat):
        pl.semaphore_signal(barrier, inc=1, device_id=at(mem, lat), device_id_type=MESH)

    greet(2 * (above % ZLO) + c, 2 * xy + above // ZLO)
    greet(2 * (below % ZLO) + c, 2 * xy + below // ZLO)
    greet(twin, j)

    def greet_lat(k, carry):
        other = (j + k) % LAT
        greet(i, other)
        greet(twin, other)
        return carry

    lax.fori_loop(1, LAT, greet_lat, 0)

    def greet_mem(k, carry):
        other = (zl + k) % ZLO
        greet(2 * other, j)
        greet(2 * other + 1, j)
        return carry

    lax.fori_loop(1, ZLO, greet_mem, 0)
    for q in range(QUARTERS):
        held = lon_ref[BAND_PAD * q : min(BAND_PAD * (q + 1), LON_BLOCK), :].astype(jnp.float32)
        if held.shape[0] < BAND_PAD:
            held = jnp.concatenate([held, jnp.zeros((BAND_PAD - held.shape[0], NLON), jnp.float32)], axis=0)
        lon_all[i, q] = held.astype(jnp.bfloat16)
    lat_rows = lat_ref[...].astype(jnp.float32)
    for b in range(2):
        held = jnp.concatenate(
            [lat_rows[BAND * b : BAND * (b + 1)], jnp.zeros((BAND_PAD - BAND, NLAT), jnp.float32)], axis=0
        )
        lat_all[i, b] = held.astype(jnp.bfloat16)
    pl.semaphore_wait(barrier, 3 + 2 * (LAT - 1) + 2 * (ZLO - 1))

    def ring(p, send, recv, slot, dev):
        part = lon_all.at[p, pl.ds(2 * half, 2)]
        return (
            remote(part, part, send.at[0, slot], recv.at[0, slot], dev),
            remote(lat_all.at[p, half], lat_all.at[p, half], send.at[1, slot], recv.at[1, slot], dev),
        )

    def beside(p, mine, slot):
        first, second = lon_all.at[p, 2 * mine], lon_all.at[p, 2 * mine + 1]
        third = lat_all.at[p, mine]
        return (
            remote(first, first, side_send.at[0, slot], side_recv.at[0, slot], plus_dev),
            remote(second, second, side_send.at[1, slot], side_recv.at[1, slot], minus_dev),
            remote(third, third, side_send.at[2, slot], side_recv.at[2, slot], plus_dev),
        )

    def across(p, slot):
        return (
            remote(lon_all.at[p], lon_all.at[p], twin_send.at[0, slot], twin_recv.at[0, slot], twin_dev),
            remote(lat_all.at[p], lat_all.at[p], twin_send.at[1, slot], twin_recv.at[1, slot], twin_dev),
        )

    def start(copies):
        for copy in copies:
            copy.start()

    start(ring(i, up_send, up_recv, 0, up_dev))
    start(ring(i, down_send, down_recv, 0, down_dev))
    start(across(i, zl))

    product = scale_ref[...] * field_ref[...]
    static_ext[:, STEPS : STEPS + ROWS, :] = product
    rows_send[0, :FIELDS] = product[:, :8, :]
    rows_send[1, :FIELDS] = product[:, ROWS - 8 :, :]
    for k in range(2):
        rows_send[0, FIELDS + k] = courant_ref[:8, k, :]
        rows_send[1, FIELDS + k] = courant_ref[ROWS - 8 :, k, :]
    first_row, last_row = i == 0, i == MEM - 1

    @pl.when(first_row)
    def _():
        rows_recv[0] = jnp.zeros(rows_recv.shape[1:], rows_recv.dtype)

    @pl.when(last_row)
    def _():
        rows_recv[1] = jnp.zeros(rows_recv.shape[1:], rows_recv.dtype)

    to_before = remote(rows_send.at[0], rows_recv.at[1], rim_send.at[0], rim_recv.at[1], at(jnp.maximum(i - 1, 0), j))
    to_after = remote(rows_send.at[1], rows_recv.at[0], rim_send.at[1], rim_recv.at[0], at(jnp.minimum(i + 1, MEM - 1), j))
    give_members = remote(
        gift, members.at[c], mem_send.at[0], mem_recv.at[0], twin_dev
    )

    get_control.wait()

    def place(f, carry):
        held = control_raw[f].astype(jnp.float32)
        for m in range(LOCAL):
            rows = jnp.concatenate([held[:, m, :], jnp.zeros((BAND_PAD - BAND, NLON), jnp.float32)], axis=0)
            control[m * FIELDS + f] = rows.astype(jnp.bfloat16)
        return carry

    lax.fori_loop(0, FIELDS, place, 0)

    def relay(d):
        source = (zl + ZLO - d) % ZLO
        for copy in ring(2 * source + c, up_send, up_recv, d - 1, up_dev):
            copy.wait_recv()
        if d < 4:
            start(ring(2 * source + c, up_send, up_recv, d, up_dev))
        start(beside(2 * source + c, half, source))
        if d < 4:
            source = (zl + d) % ZLO
            for copy in ring(2 * source + c, down_send, down_recv, d - 1, down_dev):
                copy.wait_recv()
            if d < 3:
                start(ring(2 * source + c, down_send, down_recv, d, down_dev))
            start(beside(2 * source + c, half, source))

    def complete(d):
        for step in (-1, 1) if d < 4 else (-1,):
            source = (zl + ZLO + step * d) % ZLO
            for copy in beside(2 * source + c, 1 - half, source):
                copy.wait_recv()
            start(across(2 * source + c, source))

    def block(n, carry):
        d = (n + 2) // 4
        r = (n + 2) % 4
        middle = (d + 3) // 4 - d // 4
        other = middle * (r // 2) + (1 - middle) * (r % 2)
        downward = middle * (r % 2)
        source = (zl + d * (2 * downward - 1) + ZLO) % ZLO
        p = 2 * source + (c + other) % 2

        for d in range(1, 5):

            @pl.when(n == (1 if d == 1 else 4 * (d - 1)))
            def _():
                relay(d)

            @pl.when(n == 4 * d - 2)
            def _():
                complete(d)

        @pl.when(other == 1)
        def _():
            for copy in across(p, source):
                copy.wait_recv()

        lon_rows = lon_all[p].reshape(QUARTERS * BAND_PAD, NLON)
        along = matmul(control[...].reshape(LOCAL * FIELDS * BAND_PAD, NLON), lon_rows, NT)
        lane = lax.broadcasted_iota(jnp.int32, (8, LANES), 1)
        sub = lax.broadcasted_iota(jnp.int32, (8, LANES), 0)
        for hh in range(ZHI):
            for cc in range(CORES):
                pieces = [
                    along[
                        BAND_PAD * (m * FIELDS + cc * HALF + f) : BAND_PAD * (m * FIELDS + cc * HALF + f + 1),
                        WIDTH * hh : WIDTH * (hh + 1),
                    ]
                    for m in range(LOCAL)
                    for f in range(HALF)
                ]
                pieces.append(jnp.zeros((BAND_PAD, FOLD), jnp.float32))
                row = jnp.concatenate(pieces, axis=1)
                last = row[:, WHOLE:]
                low, middle_rows, high = last[:8], last[8:16], last[16:]
                folded = jnp.where(lane < REST, low, pltpu.roll(middle_rows, REST, 1))
                wire = []
                for t in range(3):
                    tile = row[:, LANES * t : LANES * (t + 1)]
                    spare = jnp.where(lane < REST, pltpu.roll(high, 6 - 2 * t, 0), 0.0)
                    if t == 0:
                        for e in range(4):
                            start_lane = REST + SPARE * e
                            moved = pltpu.roll(pltpu.roll(middle_rows, start_lane - FOLD, 1), (6 - 2 * e) % 8, 0)
                            inside = jnp.logical_and(lane >= start_lane, lane < start_lane + SPARE)
                            spare = jnp.where(inside, moved, spare)
                    wire += [tile[:16], jnp.where(sub < 6, tile[16:], spare)]
                wire.append(folded)
                packed[p, hh, cc] = jnp.concatenate(wire, axis=0).astype(jnp.bfloat16)
        for hh in range(ZHI):
            for cc in range(CORES):
                mine = jnp.logical_and(p == xy, jnp.logical_and(h == hh, c == cc))

                @pl.when(mine)
                def _():
                    pltpu.make_async_copy(packed.at[p, hh, cc], spread.at[c, j], pack_recv.at[c, j]).start()

                @pl.when(jnp.logical_not(mine))
                def _():
                    remote(
                        packed.at[p, hh, cc], spread.at[c, j],
                        pack_send.at[p, hh, cc], pack_recv.at[c, j],
                        at(2 * zl + cc, 2 * p + hh),
                    ).start()

        @pl.when(n == 1)
        def _():
            @pl.when(jnp.logical_not(first_row))
            def _():
                to_before.start()

            @pl.when(jnp.logical_not(last_row))
            def _():
                to_after.start()

        return carry

    lax.fori_loop(0, MEM, block, 0)

    get_members.wait()

    def member_rows(part):
        rows = [members_raw[part * HALF + f].astype(jnp.float32)[:, m, :] for m in range(LOCAL) for f in range(HALF)]
        return jnp.concatenate(rows, axis=0).astype(jnp.bfloat16)

    gift[...] = member_rows(1 - c)
    give_members.start()
    members[c] = member_rows(c)

    @pl.when(jnp.logical_not(first_row))
    def _():
        to_after.wait_recv()
        to_before.wait_send()

    @pl.when(jnp.logical_not(last_row))
    def _():
        to_before.wait_recv()
        to_after.wait_send()

    static_ext[:, :STEPS, :] = rows_recv[0, :FIELDS, 8 - STEPS :, :]
    static_ext[:, STEPS + ROWS : ROWS_EXT, :] = rows_recv[1, :FIELDS, :STEPS, :]
    static_ext[:, ROWS_EXT:, :] = jnp.zeros((FIELDS, ROWS_PAD - ROWS_EXT, WIDTH), jnp.float32)
    wind[...] = jnp.zeros_like(wind)
    wind[:, :STEPS, STEPS : STEPS + WIDTH] = rows_recv[0, FIELDS:, 8 - STEPS :, :]
    for k in range(2):
        wind[k, STEPS : STEPS + ROWS, STEPS : STEPS + WIDTH] = courant_ref[:, k, :]
    wind[:, STEPS + ROWS : ROWS_EXT, STEPS : STEPS + WIDTH] = rows_recv[1, FIELDS:, :STEPS, :]
    for side, low in enumerate((STEPS, WIDTH)):
        wind_send[side] = jnp.concatenate([wind[k, :, low : low + STEPS] for k in range(2)], axis=1)
    west, east = (j + LAT - 1) % LAT, (j + 1) % LAT
    wind_west = remote(wind_send.at[0], wind_recv.at[1], wind_ssem.at[0], wind_rsem.at[1], at(i, west))
    wind_east = remote(wind_send.at[1], wind_recv.at[0], wind_ssem.at[1], wind_rsem.at[0], at(i, east))
    wind_west.start()
    wind_east.start()

    def select_rows(k, carry):
        row = lax.broadcasted_iota(jnp.int32, (ROWS_PAD, NLAT), 0)
        col = lax.broadcasted_iota(jnp.int32, (ROWS_PAD, NLAT), 1)
        hit = jnp.logical_and(col == row + (ROWS * k - STEPS), row < ROWS_EXT)
        expand[k] = jnp.where(hit, 1.0, 0.0).astype(jnp.bfloat16)
        return carry

    lax.fori_loop(0, MEM, select_rows, 0)
    lat_flat = lat_all[...].reshape(MEM * LAT_BLOCK, NLAT)
    rows_half = EXPANDED // 2
    for part in range(2):
        chooser = expand[part * ZLO : (part + 1) * ZLO].reshape(rows_half, NLAT)
        lat_t[part] = matmul(chooser, lat_flat, NT).astype(jnp.bfloat16)
    give_members.wait()
    for part in range(2):
        chooser = expand[part * ZLO : (part + 1) * ZLO].reshape(rows_half, NLAT)
        for s in range(CORES):
            pert_t[part, s] = matmul(chooser, members[s], NT).astype(jnp.bfloat16)

    wind_west.wait()
    wind_east.wait()
    for k in range(2):
        wind[k, :, :STEPS] = wind_recv[0, :, STEPS * k : STEPS * (k + 1)]
        wind[k, :, STEPS + WIDTH : 2 * STEPS + WIDTH] = wind_recv[1, :, STEPS * k : STEPS * (k + 1)]

    lane = lax.broadcasted_iota(jnp.int32, (8, LANES), 1)
    sub = lax.broadcasted_iota(jnp.int32, (8, LANES), 0)

    def arrived(k, carry):
        for s in range(CORES):
            remote(packed.at[0, 0, 0], spread.at[s, k], pack_send.at[0, 0, 0], pack_recv.at[s, k], twin_dev).wait_recv()
            folded = spread[s, k, 3 * BAND_PAD :, :].astype(jnp.float32)
            middle_rows = pltpu.roll(folded, FOLD, 1)
            high = jnp.zeros((8, LANES), jnp.float32)
            for t in range(3):
                spare = spread[s, k, BAND_PAD * t + 16 : BAND_PAD * (t + 1), :].astype(jnp.float32)
                pair = jnp.logical_and(sub >= 2 * t, sub < 2 * t + 2)
                high = jnp.where(pair, pltpu.roll(spare, (2 * t + 2) % 8, 0), high)
                if t == 0:
                    for e in range(4):
                        shift = (FOLD - REST - SPARE * e) % LANES
                        moved = pltpu.roll(pltpu.roll(spare, shift, 1), (2 * e + 2) % 8, 0)
                        inside = jnp.logical_and(sub >= 2 * e, sub < 2 * e + 2)
                        middle_rows = jnp.where(jnp.logical_and(inside, lane >= FOLD), moved, middle_rows)
            rest[s, k] = jnp.concatenate([folded, middle_rows, high], axis=0).astype(jnp.bfloat16)
        return carry

    lax.fori_loop(0, LAT, arrived, 0)
    for part in range(2):
        total = None
        for s in range(CORES):
            tiles = [spread[s, :, BAND_PAD * t : BAND_PAD * (t + 1), :] for t in range(3)] + [rest[s]]
            tiles = [t.reshape(LAT * BAND_PAD, LANES) for t in tiles]
            term = matmul(lat_t[part], jnp.concatenate(tiles, axis=1), NN)[:, :PACKED]
            term = term * pert_t[part, s].astype(jnp.float32)
            total = term if total is None else total + term
        summed = (total[:, :SUMMED] + total[:, SUMMED:]) * SCALE
        sum_send[part * ZLO : (part + 1) * ZLO] = summed.astype(jnp.bfloat16).reshape(ZLO, ROWS_PAD, SUMMED)

        def give(k, carry):
            owner = part * ZLO + k

            @pl.when(owner == i)
            def _():
                pltpu.make_async_copy(sum_send.at[owner], sum_recv.at[i], total_recv.at[i]).start()

            @pl.when(owner != i)
            def _():
                remote(sum_send.at[owner], sum_recv.at[i], total_send.at[owner], total_recv.at[i], at(owner, j)).start()

            return carry

        lax.fori_loop(0, ZLO, give, 0)

    def gathered(k, carry):
        remote(sum_send.at[0], sum_recv.at[k], total_send.at[0], total_recv.at[k], twin_dev).wait_recv()
        return carry

    lax.fori_loop(0, MEM, gathered, 0)
    state[...] = jnp.zeros_like(state)
    for s in range(CORES):
        ensemble = sum_recv[s].astype(jnp.float32)
        for z in range(1, ZLO):
            ensemble = ensemble + sum_recv[CORES * z + s].astype(jnp.float32)
        for f in range(HALF):
            field = ensemble[:, WIDTH * f : WIDTH * (f + 1)] + static_ext[s * HALF + f]
            state[s * HALF + f, :, STEPS : STEPS + WIDTH] = field
            inc_out[s * HALF + f] = field[STEPS : STEPS + ROWS, :]
    for side, low in enumerate((STEPS, WIDTH)):
        edge_send[side] = jnp.concatenate([state[f, :, low : low + STEPS] for f in range(FIELDS)], axis=1)
    edge_west = remote(edge_send.at[0], edge_recv.at[1], edge_ssem.at[0], edge_rsem.at[1], at(i, west))
    edge_east = remote(edge_send.at[1], edge_recv.at[0], edge_ssem.at[1], edge_rsem.at[0], at(i, east))
    edge_west.start()
    edge_east.start()

    for slot in range(4):
        for copy in ring(0, up_send, up_recv, slot, up_dev):
            copy.wait_send()
    for slot in range(3):
        for copy in ring(0, down_send, down_recv, slot, down_dev):
            copy.wait_send()

    def twins(k, carry):
        for copy in across(0, k):
            copy.wait_send()

        @pl.when(k != zl)
        def _():
            for copy in beside(0, half, k):
                copy.wait_send()

        return carry

    lax.fori_loop(0, ZLO, twins, 0)

    def packs(p, carry):
        for hh in range(ZHI):
            for cc in range(CORES):
                mine = jnp.logical_and(p == xy, jnp.logical_and(h == hh, c == cc))

                @pl.when(jnp.logical_not(mine))
                def _():
                    remote(
                        packed.at[p, hh, cc], spread.at[0, 0], pack_send.at[p, hh, cc], pack_recv.at[0, 0], twin_dev
                    ).wait_send()

        return carry

    lax.fori_loop(0, MEM, packs, 0)

    def totals(k, carry):
        @pl.when(k != i)
        def _():
            remote(sum_send.at[k], sum_recv.at[0], total_send.at[k], total_recv.at[0], twin_dev).wait_send()

        return carry

    lax.fori_loop(0, MEM, totals, 0)

    edge_west.wait()
    edge_east.wait()
    u, v = wind[0], wind[1]
    u_pos, u_neg = jnp.maximum(u, 0.0), jnp.minimum(u, 0.0)
    v_pos, v_neg = jnp.maximum(v, 0.0), jnp.minimum(v, 0.0)
    for f in range(FIELDS):
        state[f, :, :STEPS] = edge_recv[0, :, STEPS * f : STEPS * (f + 1)]
        state[f, :, STEPS + WIDTH : 2 * STEPS + WIDTH] = edge_recv[1, :, STEPS * f : STEPS * (f + 1)]

    def advance(f, carry):
        q = state[f]
        for _ in range(STEPS):
            western = pltpu.roll(q, 1, 1)
            eastern = pltpu.roll(q, q.shape[1] - 1, 1)
            southern = pltpu.roll(q, 1, 0)
            northern = pltpu.roll(q, q.shape[0] - 1, 0)
            zonal = u_pos * (q - western) + u_neg * (eastern - q)
            meridional = v_pos * (q - southern) + v_neg * (northern - q)
            q = q - zonal - meridional
        evo_out[f] = q[STEPS : STEPS + ROWS, STEPS : STEPS + WIDTH]
        return carry

    lax.fori_loop(0, FIELDS, advance, 0)


def per_device(control, perturb, lon_loc, lat_loc, static_scale, static_field, courant):
    anywhere = pl.BlockSpec(memory_space=pl.ANY)
    vmem = pl.BlockSpec(memory_space=pltpu.VMEM)
    bf16, f32 = jnp.bfloat16, jnp.float32
    dma = pltpu.SemaphoreType.DMA
    out = jax.ShapeDtypeStruct((FIELDS, ROWS, WIDTH), f32)
    return pl.pallas_call(
        kernel,
        out_shape=(out, out),
        in_specs=[anywhere] * 2 + [vmem] * 5,
        out_specs=(vmem, vmem),
        scratch_shapes=[
            pltpu.VMEM((FIELDS, BAND, LOCAL, NLON), bf16),
            pltpu.VMEM((LOCAL * FIELDS, BAND_PAD, NLON), bf16),
            pltpu.VMEM((FIELDS, WIDTH, LOCAL, NLAT), bf16),
            pltpu.VMEM((CORES, PACKED, NLAT), bf16),
            pltpu.VMEM((PACKED, NLAT), bf16),
            pltpu.VMEM((MEM, QUARTERS, BAND_PAD, NLON), bf16),
            pltpu.VMEM((MEM, 2, BAND_PAD, NLAT), bf16),
            pltpu.VMEM((XY, ZHI, CORES, WIRE_ROWS, LANES), bf16),
            pltpu.VMEM((CORES, LAT, WIRE_ROWS, LANES), bf16),
            pltpu.VMEM((MEM, ROWS_PAD, NLAT), bf16),
            pltpu.VMEM((2, EXPANDED // 2, LAT * BAND_PAD), bf16),
            pltpu.VMEM((2, CORES, EXPANDED // 2, PACKED), bf16),
            pltpu.VMEM((CORES, LAT, BAND_PAD, LANES), bf16),
            pltpu.VMEM((MEM, ROWS_PAD, SUMMED), bf16),
            pltpu.VMEM((MEM, ROWS_PAD, SUMMED), bf16),
            pltpu.VMEM((2, FIELDS + 2, 8, WIDTH), f32),
            pltpu.VMEM((2, FIELDS + 2, 8, WIDTH), f32),
            pltpu.VMEM((FIELDS, ROWS_PAD, WIDTH), f32),
            pltpu.VMEM((2, ROWS_PAD, 128), f32),
            pltpu.VMEM((2, ROWS_PAD, 2 * STEPS), f32),
            pltpu.VMEM((2, ROWS_PAD, 2 * STEPS), f32),
            pltpu.VMEM((FIELDS, ROWS_PAD, 128), f32),
            pltpu.VMEM((2, ROWS_PAD, FIELDS * STEPS), f32),
            pltpu.VMEM((2, ROWS_PAD, FIELDS * STEPS), f32),
            dma((4,)), dma((2, 4)), dma((2, 4)), dma((2, 3)), dma((2, 3)), dma((3, ZLO)), dma((3, ZLO)),
            dma((2, ZLO)), dma((2, ZLO)),
            dma((1,)), dma((1,)), dma((XY, ZHI, CORES)), dma((CORES, LAT)), dma((MEM,)), dma((MEM,)),
            dma((2,)), dma((2,)), dma((2,)), dma((2,)), dma((2,)), dma((2,)),
        ],
        compiler_params=pltpu.CompilerParams(
            collective_id=0, has_side_effects=True, vmem_limit_bytes=56 * 1024 * 1024
        ),
        name="increment",
    )(
        control.transpose(1, 2, 0, 3),
        perturb.transpose(1, 3, 0, 2),
        lon_loc.T,
        lat_loc,
        static_scale,
        static_field,
        courant.transpose(1, 0, 2),
    )


def solution(mesh):
    placed = (
        P("mem", None, "lat", None),
        P("mem", None, None, "lat"),
        P(None, "mem"),
        P("mem", None),
        P(None, "mem", "lat"),
        P(None, "mem", "lat"),
        P(None, "mem", "lat"),
    )
    return jax.shard_map(
        per_device,
        mesh=mesh,
        in_specs=placed,
        out_specs=(P(None, "mem", "lat"), P(None, "mem", "lat")),
        check_vma=False,
    )
```

```python
import functools
import math

import jax
import jax.numpy as jnp
from jax import lax
from jax.experimental import pallas as pl
from jax.experimental.pallas import tpu as pltpu
from jax.sharding import PartitionSpec as P

STEPS = 4
ZLO = 8
CORES = 2
XY = 16
ZHI = 2
MEM = ZLO * CORES
LAT = XY * ZHI
FIELDS = 10
HALF = FIELDS // 2
LOCAL = 2
NLAT = 704
NLON = 1440
BAND = NLAT // LAT
BAND_PAD = 24
WIDTH = NLON // LAT
ROWS = NLAT // MEM
ROWS_EXT = ROWS + 2 * STEPS
ROWS_PAD = 56
LON_BLOCK = NLON // MEM
LAT_BLOCK = 2 * BAND_PAD
QUARTERS = 4
LANES = 128
WHOLE = 3 * LANES
REST = LOCAL * HALF * WIDTH - WHOLE
FOLD = LANES - REST
WIRE_ROWS = 3 * BAND_PAD + 8
SPARE = REST - FOLD
PACKED = LOCAL * HALF * WIDTH
SUMMED = HALF * WIDTH
EXPANDED = MEM * ROWS_PAD
RELAY_AT = (1, 4, 8, 12)
COMPLETE_AT = (2, 6, 10, 14)
LAT_AT = (5, 7, 11, 13)
MESH = pl.DeviceIdType.MESH
SCALE = 1.0 / math.sqrt(31.0)
NT = (((1,), (1,)), ((), ()))
NN = (((1,), (0,)), ((), ()))


def matmul(a, b, dims):
    return lax.dot_general(a, b, dims, preferred_element_type=jnp.float32)


def kernel(
    control_hbm, perturb_hbm, lon_ref, lat_ref, scale_ref, field_ref, courant_ref,
    inc_out, evo_out,
    control_raw, control, members_raw, members, gift, lon_all, lat_all, packed, spread, expand, lat_t, pert_t,
    rest, sum_send, sum_recv, rows_send, rows_recv, static_ext, wind, wind_send, wind_recv,
    state, edge_send, edge_recv,
    local_sem, up_send, up_recv, down_send, down_recv, side_send, side_recv, twin_send, twin_recv,
    mem_send, mem_recv, pack_send, pack_recv, total_send, total_recv,
    rim_send, rim_recv, wind_ssem, wind_rsem, edge_ssem, edge_rsem,
):
    i = lax.axis_index("mem")
    j = lax.axis_index("lat")
    zl, c = i // 2, i % 2
    xy, h = j // 2, j % 2
    x, y = xy // 4, xy % 4
    half = (x + y) % 2
    quarter = 2 * (x % 2) + y % 2
    quarter_x, quarter_y = 2 - 2 * (x % 2) + y % 2, 2 * (x % 2) + 1 - y % 2
    lag = 1 + xy % 8
    next_x, next_y = (x + 1 + 2 * c) % 4, (y + 1 + 2 * c) % 4
    twin = 2 * zl + 1 - c
    above = (h * ZLO + zl + 1) % 16
    below = (h * ZLO + zl + 15) % 16

    def at(mem, lat):
        return {"mem": mem, "lat": lat}

    up_dev = at(2 * (above % ZLO) + c, 2 * xy + above // ZLO)
    down_dev = at(2 * (below % ZLO) + c, 2 * xy + below // ZLO)
    twin_dev = at(twin, j)
    x_dev = at(i, 2 * (4 * next_x + y) + h)
    y_dev = at(i, 2 * (4 * x + next_y) + h)
    diagonal_dev = at(i, 2 * (4 * next_x + next_y) + h)

    def remote(src, dst, ssem, rsem, dev):
        return pltpu.make_async_remote_copy(
            src_ref=src, dst_ref=dst, send_sem=ssem, recv_sem=rsem,
            device_id=dev, device_id_type=MESH,
        )

    get_control = pltpu.make_async_copy(control_hbm, control_raw, local_sem.at[0])
    get_members = pltpu.make_async_copy(perturb_hbm, members_raw, local_sem.at[1])
    get_control.start()
    get_members.start()

    barrier = pltpu.get_barrier_semaphore()

    def greet(mem, lat):
        pl.semaphore_signal(barrier, inc=1, device_id=at(mem, lat), device_id_type=MESH)

    greet(2 * (above % ZLO) + c, 2 * xy + above // ZLO)
    greet(2 * (below % ZLO) + c, 2 * xy + below // ZLO)
    greet(twin, j)

    def greet_lat(k, carry):
        other = (j + k) % LAT
        greet(i, other)
        greet(twin, other)
        return carry

    lax.fori_loop(1, LAT, greet_lat, 0)

    def greet_mem(k, carry):
        other = (zl + k) % ZLO
        greet(2 * other, j)
        greet(2 * other + 1, j)
        return carry

    lax.fori_loop(1, ZLO, greet_mem, 0)
    for q in range(QUARTERS):
        held = lon_ref[BAND_PAD * q : min(BAND_PAD * (q + 1), LON_BLOCK), :].astype(jnp.float32)
        if held.shape[0] < BAND_PAD:
            held = jnp.concatenate([held, jnp.zeros((BAND_PAD - held.shape[0], NLON), jnp.float32)], axis=0)
        lon_all[i, q] = held.astype(jnp.bfloat16)
    lat_rows = lat_ref[...].astype(jnp.float32)
    for b in range(2):
        held = jnp.concatenate(
            [lat_rows[BAND * b : BAND * (b + 1)], jnp.zeros((BAND_PAD - BAND, NLAT), jnp.float32)], axis=0
        )
        lat_all[i, b] = held.astype(jnp.bfloat16)
    pl.semaphore_wait(barrier, 3 + 2 * (LAT - 1) + 2 * (ZLO - 1))

    def ring(p, send, recv, slot, dev):
        part = lon_all.at[p, quarter]
        return remote(part, part, send.at[0, slot], recv.at[0, slot], dev)

    def lat_ring(p, send, recv, slot, dev):
        part = lat_all.at[p, half]
        return remote(part, part, send.at[1, slot], recv.at[1, slot], dev)

    def beside(p, parts, slot):
        return [
            remote(lon_all.at[p, part], lon_all.at[p, part], side_send.at[k, slot], side_recv.at[k, slot], dev)
            for k, (part, dev) in enumerate(zip(parts, (x_dev, y_dev, diagonal_dev)))
        ]

    def lat_beside(p, part, slot):
        part = lat_all.at[p, part]
        return remote(part, part, side_send.at[3, slot], side_recv.at[3, slot], x_dev)

    def across(p, slot):
        return remote(lon_all.at[p], lon_all.at[p], twin_send.at[0, slot], twin_recv.at[0, slot], twin_dev)

    def lat_across(p, slot):
        return remote(lat_all.at[p], lat_all.at[p], twin_send.at[1, slot], twin_recv.at[1, slot], twin_dev)

    def start(copies):
        for copy in copies:
            copy.start()

    ring(i, up_send, up_recv, 0, up_dev).start()
    ring(i, down_send, down_recv, 0, down_dev).start()
    across(i, zl).start()

    product = scale_ref[...] * field_ref[...]
    static_ext[:, STEPS : STEPS + ROWS, :] = product
    rows_send[0, :FIELDS] = product[:, :8, :]
    rows_send[1, :FIELDS] = product[:, ROWS - 8 :, :]
    for k in range(2):
        rows_send[0, FIELDS + k] = courant_ref[:8, k, :]
        rows_send[1, FIELDS + k] = courant_ref[ROWS - 8 :, k, :]
    first_row, last_row = i == 0, i == MEM - 1

    @pl.when(first_row)
    def _():
        rows_recv[0] = jnp.zeros(rows_recv.shape[1:], rows_recv.dtype)

    @pl.when(last_row)
    def _():
        rows_recv[1] = jnp.zeros(rows_recv.shape[1:], rows_recv.dtype)

    to_before = remote(rows_send.at[0], rows_recv.at[1], rim_send.at[0], rim_recv.at[1], at(jnp.maximum(i - 1, 0), j))
    to_after = remote(rows_send.at[1], rows_recv.at[0], rim_send.at[1], rim_recv.at[0], at(jnp.minimum(i + 1, MEM - 1), j))
    give_members = remote(
        gift, members.at[c], mem_send.at[0], mem_recv.at[0], twin_dev
    )

    get_control.wait()

    def place(f, carry):
        held = control_raw[f].astype(jnp.float32)
        for m in range(LOCAL):
            rows = jnp.concatenate([held[:, m, :], jnp.zeros((BAND_PAD - BAND, NLON), jnp.float32)], axis=0)
            control[m * FIELDS + f] = rows.astype(jnp.bfloat16)
        return carry

    lax.fori_loop(0, FIELDS, place, 0)

    def relay(d, ring, share):
        source = (zl + ZLO - d) % ZLO
        ring(2 * source + c, up_send, up_recv, d - 1, up_dev).wait_recv()
        if d < 4:
            ring(2 * source + c, up_send, up_recv, d, up_dev).start()
        share(2 * source + c, source)
        if d < 4:
            source = (zl + d) % ZLO
            ring(2 * source + c, down_send, down_recv, d - 1, down_dev).wait_recv()
            if d < 3:
                ring(2 * source + c, down_send, down_recv, d, down_dev).start()
            share(2 * source + c, source)

    def complete(d):
        for step in (-1, 1) if d < 4 else (-1,):
            source = (zl + ZLO + step * d) % ZLO
            for copy in beside(2 * source + c, (quarter_x, quarter_y, 3 - quarter), source):
                copy.wait_recv()
            across(2 * source + c, source).start()

    def chosen(n):
        d = (n + 2) // 4
        r = (n + 2) % 4
        middle = (d + 3) // 4 - d // 4
        other = middle * (r // 2) + (1 - middle) * (r % 2)
        downward = middle * (r % 2)
        source = (zl + d * (2 * downward - 1) + ZLO) % ZLO
        return 2 * source + (c + other) % 2, source, other

    def near(n):
        p, _, _ = chosen(n)
        for cc in range(CORES):
            mine = jnp.logical_and(p == xy, c == cc)

            @pl.when(mine)
            def _():
                pltpu.make_async_copy(packed.at[p, h, cc], spread.at[c, j], pack_recv.at[c, j]).start()

            @pl.when(jnp.logical_not(mine))
            def _():
                remote(
                    packed.at[p, h, cc], spread.at[c, j], pack_send.at[p, h, cc], pack_recv.at[c, j],
                    at(2 * zl + cc, 2 * p + h),
                ).start()

    def block(n, carry):
        p, source, other = chosen(n)

        for d in range(1, 5):

            @pl.when(n == RELAY_AT[d - 1])
            def _():
                relay(d, ring, lambda p, k: start(beside(p, (quarter, quarter, quarter), k)))

            @pl.when(n == COMPLETE_AT[d - 1])
            def _():
                complete(d)

            @pl.when(n == LAT_AT[d - 1])
            def _():
                if d == 1:
                    lat_ring(i, up_send, up_recv, 0, up_dev).start()
                    lat_ring(i, down_send, down_recv, 0, down_dev).start()
                    lat_across(i, zl).start()
                else:
                    relay(d - 1, lat_ring, lambda p, k: lat_beside(p, half, k).start())

        @pl.when(other == 1)
        def _():
            across(p, source).wait_recv()

        lon_rows = lon_all[p].reshape(QUARTERS * BAND_PAD, NLON)
        along = matmul(control[...].reshape(LOCAL * FIELDS * BAND_PAD, NLON), lon_rows, NT)
        lane = lax.broadcasted_iota(jnp.int32, (8, LANES), 1)
        sub = lax.broadcasted_iota(jnp.int32, (8, LANES), 0)
        for hh in range(ZHI):
            for cc in range(CORES):
                pieces = [
                    along[
                        BAND_PAD * (m * FIELDS + cc * HALF + f) : BAND_PAD * (m * FIELDS + cc * HALF + f + 1),
                        WIDTH * hh : WIDTH * (hh + 1),
                    ]
                    for m in range(LOCAL)
                    for f in range(HALF)
                ]
                pieces.append(jnp.zeros((BAND_PAD, FOLD), jnp.float32))
                row = jnp.concatenate(pieces, axis=1)
                last = row[:, WHOLE:]
                low, middle_rows, high = last[:8], last[8:16], last[16:]
                folded = jnp.where(lane < REST, low, pltpu.roll(middle_rows, REST, 1))
                wire = []
                for t in range(3):
                    tile = row[:, LANES * t : LANES * (t + 1)]
                    spare = jnp.where(lane < REST, pltpu.roll(high, 6 - 2 * t, 0), 0.0)
                    if t == 0:
                        for e in range(4):
                            start_lane = REST + SPARE * e
                            moved = pltpu.roll(pltpu.roll(middle_rows, start_lane - FOLD, 1), (6 - 2 * e) % 8, 0)
                            inside = jnp.logical_and(lane >= start_lane, lane < start_lane + SPARE)
                            spare = jnp.where(inside, moved, spare)
                    wire += [tile[:16], jnp.where(sub < 6, tile[16:], spare)]
                wire.append(folded)
                packed[p, hh, cc] = jnp.concatenate(wire, axis=0).astype(jnp.bfloat16)
        for cc in range(CORES):
            remote(
                packed.at[p, 1 - h, cc], spread.at[c, j], pack_send.at[p, 1 - h, cc], pack_recv.at[c, j],
                at(2 * zl + cc, 2 * p + 1 - h),
            ).start()

        @pl.when(n >= lag)
        def _():
            near(n - lag)

        @pl.when(n == 1)
        def _():
            @pl.when(jnp.logical_not(first_row))
            def _():
                to_before.start()

            @pl.when(jnp.logical_not(last_row))
            def _():
                to_after.start()

        return carry

    lax.fori_loop(0, MEM, block, 0)

    def late(k, carry):
        near(MEM - lag + k)
        return carry

    lax.fori_loop(0, lag, late, 0)

    relay(4, lat_ring, lambda p, k: lat_beside(p, half, k).start())
    get_members.wait()

    def member_rows(part):
        rows = [members_raw[part * HALF + f].astype(jnp.float32)[:, m, :] for m in range(LOCAL) for f in range(HALF)]
        return jnp.concatenate(rows, axis=0).astype(jnp.bfloat16)

    gift[...] = member_rows(1 - c)
    give_members.start()
    members[c] = member_rows(c)

    @pl.when(jnp.logical_not(first_row))
    def _():
        to_after.wait_recv()
        to_before.wait_send()

    @pl.when(jnp.logical_not(last_row))
    def _():
        to_before.wait_recv()
        to_after.wait_send()

    static_ext[:, :STEPS, :] = rows_recv[0, :FIELDS, 8 - STEPS :, :]
    static_ext[:, STEPS + ROWS : ROWS_EXT, :] = rows_recv[1, :FIELDS, :STEPS, :]
    static_ext[:, ROWS_EXT:, :] = jnp.zeros((FIELDS, ROWS_PAD - ROWS_EXT, WIDTH), jnp.float32)
    wind[...] = jnp.zeros_like(wind)
    wind[:, :STEPS, STEPS : STEPS + WIDTH] = rows_recv[0, FIELDS:, 8 - STEPS :, :]
    for k in range(2):
        wind[k, STEPS : STEPS + ROWS, STEPS : STEPS + WIDTH] = courant_ref[:, k, :]
    wind[:, STEPS + ROWS : ROWS_EXT, STEPS : STEPS + WIDTH] = rows_recv[1, FIELDS:, :STEPS, :]
    for side, low in enumerate((STEPS, WIDTH)):
        wind_send[side] = jnp.concatenate([wind[k, :, low : low + STEPS] for k in range(2)], axis=1)
    west, east = (j + LAT - 1) % LAT, (j + 1) % LAT
    wind_west = remote(wind_send.at[0], wind_recv.at[1], wind_ssem.at[0], wind_rsem.at[1], at(i, west))
    wind_east = remote(wind_send.at[1], wind_recv.at[0], wind_ssem.at[1], wind_rsem.at[0], at(i, east))
    wind_west.start()
    wind_east.start()

    def select_rows(k, carry):
        row = lax.broadcasted_iota(jnp.int32, (ROWS_PAD, NLAT), 0)
        col = lax.broadcasted_iota(jnp.int32, (ROWS_PAD, NLAT), 1)
        hit = jnp.logical_and(col == row + (ROWS * k - STEPS), row < ROWS_EXT)
        expand[k] = jnp.where(hit, 1.0, 0.0).astype(jnp.bfloat16)
        return carry

    lax.fori_loop(0, MEM, select_rows, 0)

    def lat_complete(k, carry):
        @pl.when(k != zl)
        def _():
            lat_beside(2 * k + c, 1 - half, k).wait_recv()
            lat_across(2 * k + c, k).start()

        return carry

    lax.fori_loop(0, ZLO, lat_complete, 0)

    def lat_arrived(k, carry):
        lat_across(2 * k + 1 - c, k).wait_recv()
        return carry

    lax.fori_loop(0, ZLO, lat_arrived, 0)
    lat_flat = lat_all[...].reshape(MEM * LAT_BLOCK, NLAT)
    rows_half = EXPANDED // 2
    for part in range(2):
        chooser = expand[part * ZLO : (part + 1) * ZLO].reshape(rows_half, NLAT)
        lat_t[part] = matmul(chooser, lat_flat, NT).astype(jnp.bfloat16)
    give_members.wait()
    for part in range(2):
        chooser = expand[part * ZLO : (part + 1) * ZLO].reshape(rows_half, NLAT)
        for s in range(CORES):
            pert_t[part, s] = matmul(chooser, members[s], NT).astype(jnp.bfloat16)

    wind_west.wait()
    wind_east.wait()
    for k in range(2):
        wind[k, :, :STEPS] = wind_recv[0, :, STEPS * k : STEPS * (k + 1)]
        wind[k, :, STEPS + WIDTH : 2 * STEPS + WIDTH] = wind_recv[1, :, STEPS * k : STEPS * (k + 1)]

    lane = lax.broadcasted_iota(jnp.int32, (8, LANES), 1)
    sub = lax.broadcasted_iota(jnp.int32, (8, LANES), 0)

    def arrived(k, carry):
        for s in range(CORES):
            remote(packed.at[0, 0, 0], spread.at[s, k], pack_send.at[0, 0, 0], pack_recv.at[s, k], twin_dev).wait_recv()
            folded = spread[s, k, 3 * BAND_PAD :, :].astype(jnp.float32)
            middle_rows = pltpu.roll(folded, FOLD, 1)
            high = jnp.zeros((8, LANES), jnp.float32)
            for t in range(3):
                spare = spread[s, k, BAND_PAD * t + 16 : BAND_PAD * (t + 1), :].astype(jnp.float32)
                pair = jnp.logical_and(sub >= 2 * t, sub < 2 * t + 2)
                high = jnp.where(pair, pltpu.roll(spare, (2 * t + 2) % 8, 0), high)
                if t == 0:
                    for e in range(4):
                        shift = (FOLD - REST - SPARE * e) % LANES
                        moved = pltpu.roll(pltpu.roll(spare, shift, 1), (2 * e + 2) % 8, 0)
                        inside = jnp.logical_and(sub >= 2 * e, sub < 2 * e + 2)
                        middle_rows = jnp.where(jnp.logical_and(inside, lane >= FOLD), moved, middle_rows)
            rest[s, k] = jnp.concatenate([folded, middle_rows, high], axis=0).astype(jnp.bfloat16)
        return carry

    lax.fori_loop(0, LAT, arrived, 0)
    for part in range(2):
        total = None
        for s in range(CORES):
            tiles = [spread[s, :, BAND_PAD * t : BAND_PAD * (t + 1), :] for t in range(3)] + [rest[s]]
            tiles = [t.reshape(LAT * BAND_PAD, LANES) for t in tiles]
            term = matmul(lat_t[part], jnp.concatenate(tiles, axis=1), NN)[:, :PACKED]
            term = term * pert_t[part, s].astype(jnp.float32)
            total = term if total is None else total + term
        summed = (total[:, :SUMMED] + total[:, SUMMED:]) * SCALE
        sum_send[part * ZLO : (part + 1) * ZLO] = summed.astype(jnp.bfloat16).reshape(ZLO, ROWS_PAD, SUMMED)

    def give(k, carry):
        for step in (1, -1):
            other = zl + step * (ZLO - 1 - k)

            @pl.when(jnp.logical_and(other >= 0, other < ZLO))
            def _():
                for cc in range(CORES):
                    owner = 2 * other + cc
                    remote(
                        sum_send.at[owner], sum_recv.at[i], total_send.at[owner], total_recv.at[i], at(owner, j)
                    ).start()

        return carry

    lax.fori_loop(0, ZLO - 1, give, 0)
    pltpu.make_async_copy(sum_send.at[i], sum_recv.at[i], total_recv.at[i]).start()
    remote(sum_send.at[twin], sum_recv.at[i], total_send.at[twin], total_recv.at[i], twin_dev).start()

    def gathered(k, carry):
        remote(sum_send.at[0], sum_recv.at[k], total_send.at[0], total_recv.at[k], twin_dev).wait_recv()
        return carry

    lax.fori_loop(0, MEM, gathered, 0)
    state[...] = jnp.zeros_like(state)
    for s in range(CORES):
        ensemble = sum_recv[s].astype(jnp.float32)
        for z in range(1, ZLO):
            ensemble = ensemble + sum_recv[CORES * z + s].astype(jnp.float32)
        for f in range(HALF):
            field = ensemble[:, WIDTH * f : WIDTH * (f + 1)] + static_ext[s * HALF + f]
            state[s * HALF + f, :, STEPS : STEPS + WIDTH] = field
            inc_out[s * HALF + f] = field[STEPS : STEPS + ROWS, :]
    for side, low in enumerate((STEPS, WIDTH)):
        edge_send[side] = jnp.concatenate([state[f, :, low : low + STEPS] for f in range(FIELDS)], axis=1)
    edge_west = remote(edge_send.at[0], edge_recv.at[1], edge_ssem.at[0], edge_rsem.at[1], at(i, west))
    edge_east = remote(edge_send.at[1], edge_recv.at[0], edge_ssem.at[1], edge_rsem.at[0], at(i, east))
    edge_west.start()
    edge_east.start()

    for send in (ring, lat_ring):
        for slot in range(4):
            send(0, up_send, up_recv, slot, up_dev).wait_send()
        for slot in range(3):
            send(0, down_send, down_recv, slot, down_dev).wait_send()

    def twins(k, carry):
        across(0, k).wait_send()
        lat_across(0, k).wait_send()

        @pl.when(k != zl)
        def _():
            for copy in beside(0, (quarter, quarter, quarter), k):
                copy.wait_send()
            lat_beside(0, half, k).wait_send()

        return carry

    lax.fori_loop(0, ZLO, twins, 0)

    def packs(p, carry):
        for hh in range(ZHI):
            for cc in range(CORES):
                mine = jnp.logical_and(p == xy, jnp.logical_and(h == hh, c == cc))

                @pl.when(jnp.logical_not(mine))
                def _():
                    remote(
                        packed.at[p, hh, cc], spread.at[0, 0], pack_send.at[p, hh, cc], pack_recv.at[0, 0], twin_dev
                    ).wait_send()

        return carry

    lax.fori_loop(0, MEM, packs, 0)

    def totals(k, carry):
        @pl.when(k != i)
        def _():
            remote(sum_send.at[k], sum_recv.at[0], total_send.at[k], total_recv.at[0], twin_dev).wait_send()

        return carry

    lax.fori_loop(0, MEM, totals, 0)

    edge_west.wait()
    edge_east.wait()
    u, v = wind[0], wind[1]
    u_pos, u_neg = jnp.maximum(u, 0.0), jnp.minimum(u, 0.0)
    v_pos, v_neg = jnp.maximum(v, 0.0), jnp.minimum(v, 0.0)
    for f in range(FIELDS):
        state[f, :, :STEPS] = edge_recv[0, :, STEPS * f : STEPS * (f + 1)]
        state[f, :, STEPS + WIDTH : 2 * STEPS + WIDTH] = edge_recv[1, :, STEPS * f : STEPS * (f + 1)]

    def advance(f, carry):
        q = state[f]
        for _ in range(STEPS):
            western = pltpu.roll(q, 1, 1)
            eastern = pltpu.roll(q, q.shape[1] - 1, 1)
            southern = pltpu.roll(q, 1, 0)
            northern = pltpu.roll(q, q.shape[0] - 1, 0)
            zonal = u_pos * (q - western) + u_neg * (eastern - q)
            meridional = v_pos * (q - southern) + v_neg * (northern - q)
            q = q - zonal - meridional
        evo_out[f] = q[STEPS : STEPS + ROWS, STEPS : STEPS + WIDTH]
        return carry

    lax.fori_loop(0, FIELDS, advance, 0)


def per_device(control, perturb, lon_loc, lat_loc, static_scale, static_field, courant):
    anywhere = pl.BlockSpec(memory_space=pl.ANY)
    vmem = pl.BlockSpec(memory_space=pltpu.VMEM)
    bf16, f32 = jnp.bfloat16, jnp.float32
    dma = pltpu.SemaphoreType.DMA
    out = jax.ShapeDtypeStruct((FIELDS, ROWS, WIDTH), f32)
    return pl.pallas_call(
        kernel,
        out_shape=(out, out),
        in_specs=[anywhere] * 2 + [vmem] * 5,
        out_specs=(vmem, vmem),
        scratch_shapes=[
            pltpu.VMEM((FIELDS, BAND, LOCAL, NLON), bf16),
            pltpu.VMEM((LOCAL * FIELDS, BAND_PAD, NLON), bf16),
            pltpu.VMEM((FIELDS, WIDTH, LOCAL, NLAT), bf16),
            pltpu.VMEM((CORES, PACKED, NLAT), bf16),
            pltpu.VMEM((PACKED, NLAT), bf16),
            pltpu.VMEM((MEM, QUARTERS, BAND_PAD, NLON), bf16),
            pltpu.VMEM((MEM, 2, BAND_PAD, NLAT), bf16),
            pltpu.VMEM((XY, ZHI, CORES, WIRE_ROWS, LANES), bf16),
            pltpu.VMEM((CORES, LAT, WIRE_ROWS, LANES), bf16),
            pltpu.VMEM((MEM, ROWS_PAD, NLAT), bf16),
            pltpu.VMEM((2, EXPANDED // 2, LAT * BAND_PAD), bf16),
            pltpu.VMEM((2, CORES, EXPANDED // 2, PACKED), bf16),
            pltpu.VMEM((CORES, LAT, BAND_PAD, LANES), bf16),
            pltpu.VMEM((MEM, ROWS_PAD, SUMMED), bf16),
            pltpu.VMEM((MEM, ROWS_PAD, SUMMED), bf16),
            pltpu.VMEM((2, FIELDS + 2, 8, WIDTH), f32),
            pltpu.VMEM((2, FIELDS + 2, 8, WIDTH), f32),
            pltpu.VMEM((FIELDS, ROWS_PAD, WIDTH), f32),
            pltpu.VMEM((2, ROWS_PAD, 128), f32),
            pltpu.VMEM((2, ROWS_PAD, 2 * STEPS), f32),
            pltpu.VMEM((2, ROWS_PAD, 2 * STEPS), f32),
            pltpu.VMEM((FIELDS, ROWS_PAD, 128), f32),
            pltpu.VMEM((2, ROWS_PAD, FIELDS * STEPS), f32),
            pltpu.VMEM((2, ROWS_PAD, FIELDS * STEPS), f32),
            dma((4,)), dma((2, 4)), dma((2, 4)), dma((2, 3)), dma((2, 3)), dma((4, ZLO)), dma((4, ZLO)),
            dma((2, ZLO)), dma((2, ZLO)),
            dma((1,)), dma((1,)), dma((XY, ZHI, CORES)), dma((CORES, LAT)), dma((MEM,)), dma((MEM,)),
            dma((2,)), dma((2,)), dma((2,)), dma((2,)), dma((2,)), dma((2,)),
        ],
        compiler_params=pltpu.CompilerParams(
            collective_id=0, has_side_effects=True, vmem_limit_bytes=56 * 1024 * 1024
        ),
        name="increment",
    )(
        control.transpose(1, 2, 0, 3),
        perturb.transpose(1, 3, 0, 2),
        lon_loc.T,
        lat_loc,
        static_scale,
        static_field,
        courant.transpose(1, 0, 2),
    )


def solution(mesh):
    placed = (
        P("mem", None, "lat", None),
        P("mem", None, None, "lat"),
        P(None, "mem"),
        P("mem", None),
        P(None, "mem", "lat"),
        P(None, "mem", "lat"),
        P(None, "mem", "lat"),
    )
    return jax.shard_map(
        per_device,
        mesh=mesh,
        in_specs=placed,
        out_specs=(P(None, "mem", "lat"), P(None, "mem", "lat")),
        check_vma=False,
    )
```

```python
import functools
import math

import jax
import jax.numpy as jnp
from jax import lax
from jax.experimental import pallas as pl
from jax.experimental.pallas import tpu as pltpu
from jax.sharding import PartitionSpec as P

STEPS = 4
ZLO = 8
CORES = 2
XY = 16
ZHI = 2
MEM = ZLO * CORES
LAT = XY * ZHI
FIELDS = 10
HALF = FIELDS // 2
LOCAL = 2
NLAT = 704
NLON = 1440
BAND = NLAT // LAT
BAND_PAD = 24
WIDTH = NLON // LAT
ROWS = NLAT // MEM
ROWS_EXT = ROWS + 2 * STEPS
ROWS_PAD = 56
LON_BLOCK = NLON // MEM
LAT_BLOCK = 2 * BAND_PAD
QUARTERS = 4
LANES = 128
WHOLE = 3 * LANES
REST = LOCAL * HALF * WIDTH - WHOLE
FOLD = LANES - REST
WIRE_ROWS = 3 * BAND_PAD + 8
SPARE = REST - FOLD
SENT_ROWS = 48
EDGE = HALF * WIDTH - LANES
GAP = LANES - EDGE
PACKED = LOCAL * HALF * WIDTH
SUMMED = HALF * WIDTH
EXPANDED = MEM * ROWS_PAD
RELAY_AT = (1, 4, 8, 12)
COMPLETE_AT = (2, 6, 10, 14)
LAT_AT = (5, 7, 11, 13)
MESH = pl.DeviceIdType.MESH
SCALE = 1.0 / math.sqrt(31.0)
NT = (((1,), (1,)), ((), ()))
NN = (((1,), (0,)), ((), ()))


def matmul(a, b, dims):
    return lax.dot_general(a, b, dims, preferred_element_type=jnp.float32)


def kernel(
    control_hbm, perturb_hbm, lon_ref, lat_ref, scale_ref, field_ref, courant_ref,
    inc_out, evo_out,
    control_raw, control, members_raw, members, gift, lon_all, lat_all, packed, spread, expand, lat_t, pert_t,
    rest, sum_send, sum_recv, rows_send, rows_recv, static_ext, wind, wind_send, wind_recv,
    state, edge_send, edge_recv,
    local_sem, up_send, up_recv, down_send, down_recv, side_send, side_recv, twin_send, twin_recv,
    mem_send, mem_recv, pack_send, pack_recv, total_send, total_recv,
    rim_send, rim_recv, wind_ssem, wind_rsem, edge_ssem, edge_rsem,
):
    i = lax.axis_index("mem")
    j = lax.axis_index("lat")
    zl, c = i // 2, i % 2
    xy, h = j // 2, j % 2
    x, y = xy // 4, xy % 4
    half = (x + y) % 2
    quarter = 2 * (x % 2) + y % 2
    quarter_x, quarter_y = 2 - 2 * (x % 2) + y % 2, 2 * (x % 2) + 1 - y % 2
    lag = 1 + xy % 8
    next_x, next_y = (x + 1 + 2 * c) % 4, (y + 1 + 2 * c) % 4
    twin = 2 * zl + 1 - c
    above = (h * ZLO + zl + 1) % 16
    below = (h * ZLO + zl + 15) % 16

    def at(mem, lat):
        return {"mem": mem, "lat": lat}

    up_dev = at(2 * (above % ZLO) + c, 2 * xy + above // ZLO)
    down_dev = at(2 * (below % ZLO) + c, 2 * xy + below // ZLO)
    twin_dev = at(twin, j)
    x_dev = at(i, 2 * (4 * next_x + y) + h)
    y_dev = at(i, 2 * (4 * x + next_y) + h)
    diagonal_dev = at(i, 2 * (4 * next_x + next_y) + h)

    def remote(src, dst, ssem, rsem, dev):
        return pltpu.make_async_remote_copy(
            src_ref=src, dst_ref=dst, send_sem=ssem, recv_sem=rsem,
            device_id=dev, device_id_type=MESH,
        )

    get_control = pltpu.make_async_copy(control_hbm, control_raw, local_sem.at[0])
    get_members = pltpu.make_async_copy(perturb_hbm, members_raw, local_sem.at[1])
    get_control.start()
    get_members.start()

    barrier = pltpu.get_barrier_semaphore()

    def greet(mem, lat):
        pl.semaphore_signal(barrier, inc=1, device_id=at(mem, lat), device_id_type=MESH)

    greet(2 * (above % ZLO) + c, 2 * xy + above // ZLO)
    greet(2 * (below % ZLO) + c, 2 * xy + below // ZLO)
    greet(twin, j)

    def greet_lat(k, carry):
        other = (j + k) % LAT
        greet(i, other)
        greet(twin, other)
        return carry

    lax.fori_loop(1, LAT, greet_lat, 0)

    def greet_mem(k, carry):
        other = (zl + k) % ZLO
        greet(2 * other, j)
        greet(2 * other + 1, j)
        return carry

    lax.fori_loop(1, ZLO, greet_mem, 0)
    for q in range(QUARTERS):
        held = lon_ref[BAND_PAD * q : min(BAND_PAD * (q + 1), LON_BLOCK), :].astype(jnp.float32)
        if held.shape[0] < BAND_PAD:
            held = jnp.concatenate([held, jnp.zeros((BAND_PAD - held.shape[0], NLON), jnp.float32)], axis=0)
        lon_all[i, q] = held.astype(jnp.bfloat16)
    lat_rows = lat_ref[...].astype(jnp.float32)
    for b in range(2):
        held = jnp.concatenate(
            [lat_rows[BAND * b : BAND * (b + 1)], jnp.zeros((BAND_PAD - BAND, NLAT), jnp.float32)], axis=0
        )
        lat_all[i, b] = held.astype(jnp.bfloat16)
    product = scale_ref[...] * field_ref[...]
    static_ext[:, STEPS : STEPS + ROWS, :] = product
    rows_send[0, :FIELDS] = product[:, :8, :]
    rows_send[1, :FIELDS] = product[:, ROWS - 8 :, :]
    for k in range(2):
        rows_send[0, FIELDS + k] = courant_ref[:8, k, :]
        rows_send[1, FIELDS + k] = courant_ref[ROWS - 8 :, k, :]
    first_row, last_row = i == 0, i == MEM - 1

    @pl.when(first_row)
    def _():
        rows_recv[0] = jnp.zeros(rows_recv.shape[1:], rows_recv.dtype)

    @pl.when(last_row)
    def _():
        rows_recv[1] = jnp.zeros(rows_recv.shape[1:], rows_recv.dtype)

    get_control.wait()

    def place(f, carry):
        held = control_raw[f].astype(jnp.float32)
        for m in range(LOCAL):
            rows = jnp.concatenate([held[:, m, :], jnp.zeros((BAND_PAD - BAND, NLON), jnp.float32)], axis=0)
            control[m * FIELDS + f] = rows.astype(jnp.bfloat16)
        return carry

    lax.fori_loop(0, FIELDS, place, 0)

    pl.semaphore_wait(barrier, 3 + 2 * (LAT - 1) + 2 * (ZLO - 1))

    def ring(p, send, recv, slot, dev):
        part = lon_all.at[p, quarter]
        return remote(part, part, send.at[0, slot], recv.at[0, slot], dev)

    def lat_ring(p, send, recv, slot, dev):
        part = lat_all.at[p, half]
        return remote(part, part, send.at[1, slot], recv.at[1, slot], dev)

    def beside(p, parts, slot):
        return [
            remote(lon_all.at[p, part], lon_all.at[p, part], side_send.at[k, slot], side_recv.at[k, slot], dev)
            for k, (part, dev) in enumerate(zip(parts, (x_dev, y_dev, diagonal_dev)))
        ]

    def lat_beside(p, part, slot):
        part = lat_all.at[p, part]
        return remote(part, part, side_send.at[3, slot], side_recv.at[3, slot], x_dev)

    def across(p, slot):
        return remote(lon_all.at[p], lon_all.at[p], twin_send.at[0, slot], twin_recv.at[0, slot], twin_dev)

    def lat_across(p, slot):
        return remote(lat_all.at[p], lat_all.at[p], twin_send.at[1, slot], twin_recv.at[1, slot], twin_dev)

    def start(copies):
        for copy in copies:
            copy.start()

    ring(i, up_send, up_recv, 0, up_dev).start()
    ring(i, down_send, down_recv, 0, down_dev).start()
    across(i, zl).start()

    to_before = remote(rows_send.at[0], rows_recv.at[1], rim_send.at[0], rim_recv.at[1], at(jnp.maximum(i - 1, 0), j))
    to_after = remote(rows_send.at[1], rows_recv.at[0], rim_send.at[1], rim_recv.at[0], at(jnp.minimum(i + 1, MEM - 1), j))
    give_members = remote(
        gift, members.at[c], mem_send.at[0], mem_recv.at[0], twin_dev
    )

    def relay(d, ring, share):
        source = (zl + ZLO - d) % ZLO
        ring(2 * source + c, up_send, up_recv, d - 1, up_dev).wait_recv()
        if d < 4:
            ring(2 * source + c, up_send, up_recv, d, up_dev).start()
        share(2 * source + c, source)
        if d < 4:
            source = (zl + d) % ZLO
            ring(2 * source + c, down_send, down_recv, d - 1, down_dev).wait_recv()
            if d < 3:
                ring(2 * source + c, down_send, down_recv, d, down_dev).start()
            share(2 * source + c, source)

    def complete(d):
        for step in (-1, 1) if d < 4 else (-1,):
            source = (zl + ZLO + step * d) % ZLO
            for copy in beside(2 * source + c, (quarter_x, quarter_y, 3 - quarter), source):
                copy.wait_recv()
            across(2 * source + c, source).start()

    def chosen(n):
        d = (n + 2) // 4
        r = (n + 2) % 4
        middle = (d + 3) // 4 - d // 4
        other = middle * (r // 2) + (1 - middle) * (r % 2)
        downward = middle * (r % 2)
        source = (zl + d * (2 * downward - 1) + ZLO) % ZLO
        return 2 * source + (c + other) % 2, source, other

    def near(n):
        p, _, _ = chosen(n)
        for cc in range(CORES):
            mine = jnp.logical_and(p == xy, c == cc)

            @pl.when(mine)
            def _():
                pltpu.make_async_copy(packed.at[p, h, cc], spread.at[c, j], pack_recv.at[c, j]).start()

            @pl.when(jnp.logical_not(mine))
            def _():
                remote(
                    packed.at[p, h, cc], spread.at[c, j], pack_send.at[p, h, cc], pack_recv.at[c, j],
                    at(2 * zl + cc, 2 * p + h),
                ).start()

    west, east = (j + LAT - 1) % LAT, (j + 1) % LAT
    wind_west = remote(wind_send.at[0], wind_recv.at[1], wind_ssem.at[0], wind_rsem.at[1], at(i, west))
    wind_east = remote(wind_send.at[1], wind_recv.at[0], wind_ssem.at[1], wind_rsem.at[0], at(i, east))

    def member_rows(part):
        rows = [members_raw[part * HALF + f].astype(jnp.float32)[:, m, :] for m in range(LOCAL) for f in range(HALF)]
        return jnp.concatenate(rows, axis=0).astype(jnp.bfloat16)

    def share_members():
        get_members.wait()
        gift[...] = member_rows(1 - c)
        give_members.start()
        members[c] = member_rows(c)

    def share_wind():
        @pl.when(jnp.logical_not(first_row))
        def _():
            to_after.wait_recv()
            to_before.wait_send()

        @pl.when(jnp.logical_not(last_row))
        def _():
            to_before.wait_recv()
            to_after.wait_send()

        static_ext[:, :STEPS, :] = rows_recv[0, :FIELDS, 8 - STEPS :, :]
        static_ext[:, STEPS + ROWS : ROWS_EXT, :] = rows_recv[1, :FIELDS, :STEPS, :]
        static_ext[:, ROWS_EXT:, :] = jnp.zeros((FIELDS, ROWS_PAD - ROWS_EXT, WIDTH), jnp.float32)
        wind[...] = jnp.zeros_like(wind)
        wind[:, :STEPS, STEPS : STEPS + WIDTH] = rows_recv[0, FIELDS:, 8 - STEPS :, :]
        for k in range(2):
            wind[k, STEPS : STEPS + ROWS, STEPS : STEPS + WIDTH] = courant_ref[:, k, :]
        wind[:, STEPS + ROWS : ROWS_EXT, STEPS : STEPS + WIDTH] = rows_recv[1, FIELDS:, :STEPS, :]
        for side, low in enumerate((STEPS, WIDTH)):
            wind_send[side] = jnp.concatenate([wind[k, :, low : low + STEPS] for k in range(2)], axis=1)
        wind_west.start()
        wind_east.start()

    def block(n, carry):
        p, source, other = chosen(n)

        for d in range(1, 5):

            @pl.when(n == RELAY_AT[d - 1])
            def _():
                relay(d, ring, lambda p, k: start(beside(p, (quarter, quarter, quarter), k)))

            @pl.when(n == COMPLETE_AT[d - 1])
            def _():
                complete(d)

            @pl.when(n == LAT_AT[d - 1])
            def _():
                if d == 1:
                    lat_ring(i, up_send, up_recv, 0, up_dev).start()
                    lat_ring(i, down_send, down_recv, 0, down_dev).start()
                    lat_across(i, zl).start()
                else:
                    relay(d - 1, lat_ring, lambda p, k: lat_beside(p, half, k).start())

        @pl.when(other == 1)
        def _():
            across(p, source).wait_recv()

        lon_rows = lon_all[p].reshape(QUARTERS * BAND_PAD, NLON)
        along = matmul(control[...].reshape(LOCAL * FIELDS * BAND_PAD, NLON), lon_rows, NT)
        lane = lax.broadcasted_iota(jnp.int32, (8, LANES), 1)
        sub = lax.broadcasted_iota(jnp.int32, (8, LANES), 0)
        for hh in range(ZHI):
            for cc in range(CORES):
                pieces = [
                    along[
                        BAND_PAD * (m * FIELDS + cc * HALF + f) : BAND_PAD * (m * FIELDS + cc * HALF + f + 1),
                        WIDTH * hh : WIDTH * (hh + 1),
                    ]
                    for m in range(LOCAL)
                    for f in range(HALF)
                ]
                pieces.append(jnp.zeros((BAND_PAD, FOLD), jnp.float32))
                row = jnp.concatenate(pieces, axis=1)
                last = row[:, WHOLE:]
                low, middle_rows, high = last[:8], last[8:16], last[16:]
                folded = jnp.where(lane < REST, low, pltpu.roll(middle_rows, REST, 1))
                wire = []
                for t in range(3):
                    tile = row[:, LANES * t : LANES * (t + 1)]
                    spare = jnp.where(lane < REST, pltpu.roll(high, 6 - 2 * t, 0), 0.0)
                    if t == 0:
                        for e in range(4):
                            start_lane = REST + SPARE * e
                            moved = pltpu.roll(pltpu.roll(middle_rows, start_lane - FOLD, 1), (6 - 2 * e) % 8, 0)
                            inside = jnp.logical_and(lane >= start_lane, lane < start_lane + SPARE)
                            spare = jnp.where(inside, moved, spare)
                    wire += [tile[:16], jnp.where(sub < 6, tile[16:], spare)]
                wire.append(folded)
                packed[p, hh, cc] = jnp.concatenate(wire, axis=0).astype(jnp.bfloat16)
        for cc in range(CORES):
            remote(
                packed.at[p, 1 - h, cc], spread.at[c, j], pack_send.at[p, 1 - h, cc], pack_recv.at[c, j],
                at(2 * zl + cc, 2 * p + 1 - h),
            ).start()

        @pl.when(n >= lag)
        def _():
            near(n - lag)

        @pl.when(n == 1)
        def _():
            @pl.when(jnp.logical_not(first_row))
            def _():
                to_before.start()

            @pl.when(jnp.logical_not(last_row))
            def _():
                to_after.start()

        @pl.when(n == 9)
        def _():
            share_wind()

        @pl.when(n == 11)
        def _():
            share_members()

        return carry

    lax.fori_loop(0, MEM, block, 0)

    def late(k, carry):
        near(MEM - lag + k)
        return carry

    lax.fori_loop(0, lag, late, 0)

    relay(4, lat_ring, lambda p, k: lat_beside(p, half, k).start())
    def select_rows(k, carry):
        row = lax.broadcasted_iota(jnp.int32, (ROWS_PAD, NLAT), 0)
        col = lax.broadcasted_iota(jnp.int32, (ROWS_PAD, NLAT), 1)
        hit = jnp.logical_and(col == row + (ROWS * k - STEPS), row < ROWS_EXT)
        expand[k] = jnp.where(hit, 1.0, 0.0).astype(jnp.bfloat16)
        return carry

    lax.fori_loop(0, MEM, select_rows, 0)

    def lat_complete(k, carry):
        @pl.when(k != zl)
        def _():
            lat_beside(2 * k + c, 1 - half, k).wait_recv()
            lat_across(2 * k + c, k).start()

        return carry

    lax.fori_loop(0, ZLO, lat_complete, 0)

    def lat_arrived(k, carry):
        lat_across(2 * k + 1 - c, k).wait_recv()
        return carry

    lax.fori_loop(0, ZLO, lat_arrived, 0)
    lat_flat = lat_all[...].reshape(MEM * LAT_BLOCK, NLAT)
    rows_half = EXPANDED // 2
    for part in range(2):
        chooser = expand[part * ZLO : (part + 1) * ZLO].reshape(rows_half, NLAT)
        lat_t[part] = matmul(chooser, lat_flat, NT).astype(jnp.bfloat16)
    give_members.wait()
    for part in range(2):
        chooser = expand[part * ZLO : (part + 1) * ZLO].reshape(rows_half, NLAT)
        for s in range(CORES):
            pert_t[part, s] = matmul(chooser, members[s], NT).astype(jnp.bfloat16)

    wind_west.wait()
    wind_east.wait()
    for k in range(2):
        wind[k, :, :STEPS] = wind_recv[0, :, STEPS * k : STEPS * (k + 1)]
        wind[k, :, STEPS + WIDTH : 2 * STEPS + WIDTH] = wind_recv[1, :, STEPS * k : STEPS * (k + 1)]

    lane = lax.broadcasted_iota(jnp.int32, (8, LANES), 1)
    sub = lax.broadcasted_iota(jnp.int32, (8, LANES), 0)

    def arrived(k, carry):
        for s in range(CORES):
            remote(packed.at[0, 0, 0], spread.at[s, k], pack_send.at[0, 0, 0], pack_recv.at[s, k], twin_dev).wait_recv()
            folded = spread[s, k, 3 * BAND_PAD :, :].astype(jnp.float32)
            middle_rows = pltpu.roll(folded, FOLD, 1)
            high = jnp.zeros((8, LANES), jnp.float32)
            for t in range(3):
                spare = spread[s, k, BAND_PAD * t + 16 : BAND_PAD * (t + 1), :].astype(jnp.float32)
                pair = jnp.logical_and(sub >= 2 * t, sub < 2 * t + 2)
                high = jnp.where(pair, pltpu.roll(spare, (2 * t + 2) % 8, 0), high)
                if t == 0:
                    for e in range(4):
                        shift = (FOLD - REST - SPARE * e) % LANES
                        moved = pltpu.roll(pltpu.roll(spare, shift, 1), (2 * e + 2) % 8, 0)
                        inside = jnp.logical_and(sub >= 2 * e, sub < 2 * e + 2)
                        middle_rows = jnp.where(jnp.logical_and(inside, lane >= FOLD), moved, middle_rows)
            rest[s, k] = jnp.concatenate([folded, middle_rows, high], axis=0).astype(jnp.bfloat16)
        return carry

    lax.fori_loop(0, LAT, arrived, 0)
    for part in range(2):
        total = None
        for s in range(CORES):
            tiles = [spread[s, :, BAND_PAD * t : BAND_PAD * (t + 1), :] for t in range(3)] + [rest[s]]
            tiles = [t.reshape(LAT * BAND_PAD, LANES) for t in tiles]
            term = matmul(lat_t[part], jnp.concatenate(tiles, axis=1), NN)[:, :PACKED]
            term = term * pert_t[part, s].astype(jnp.float32)
            total = term if total is None else total + term
        summed = (total[:, :SUMMED] + total[:, SUMMED:]) * SCALE
        summed = jnp.concatenate([summed, jnp.zeros((rows_half, GAP), jnp.float32)], axis=1)
        for k in range(ZLO):
            chunk = summed[ROWS_PAD * k : ROWS_PAD * (k + 1)]
            right = chunk[:, LANES:]
            left_end, right_end = chunk[SENT_ROWS:, :LANES], right[SENT_ROWS:]
            strips = []
            for t in range(SENT_ROWS // 8):
                strip = right[8 * t : 8 * (t + 1)]
                if t < 4:
                    if t < 3:
                        second = pltpu.roll(right_end, EDGE - GAP * t, 1)
                    else:
                        second = jnp.where(
                            lane < EDGE + 4,
                            pltpu.roll(left_end, EDGE + 4, 1),
                            pltpu.roll(right_end, EDGE + 4 - 3 * GAP, 1),
                        )
                    first = pltpu.roll(left_end, (EDGE - GAP * t) % LANES, 1)
                    spare = jnp.where(sub < 4, first, pltpu.roll(second, 4, 0))
                    strip = jnp.where(lane < EDGE, strip, spare)
                strips.append(strip)
            sent = jnp.concatenate([chunk[:SENT_ROWS, :LANES], jnp.concatenate(strips, axis=0)], axis=1)
            sum_send[part * ZLO + k] = sent.astype(jnp.bfloat16)

    def give(k, carry):
        for step in (1, -1):
            other = zl + step * (ZLO - 1 - k)

            @pl.when(jnp.logical_and(other >= 0, other < ZLO))
            def _():
                for cc in range(CORES):
                    owner = 2 * other + cc
                    remote(
                        sum_send.at[owner], sum_recv.at[i], total_send.at[owner], total_recv.at[i], at(owner, j)
                    ).start()

        return carry

    lax.fori_loop(0, ZLO - 1, give, 0)
    pltpu.make_async_copy(sum_send.at[i], sum_recv.at[i], total_recv.at[i]).start()
    remote(sum_send.at[twin], sum_recv.at[i], total_send.at[twin], total_recv.at[i], twin_dev).start()

    def gathered(k, carry):
        remote(sum_send.at[0], sum_recv.at[k], total_send.at[0], total_recv.at[k], twin_dev).wait_recv()
        return carry

    lax.fori_loop(0, MEM, gathered, 0)
    state[...] = jnp.zeros_like(state)
    for s in range(CORES):
        ensemble = sum_recv[s].astype(jnp.float32)
        for z in range(1, ZLO):
            ensemble = ensemble + sum_recv[CORES * z + s].astype(jnp.float32)
        left_end = jnp.zeros((8, LANES), jnp.float32)
        right_end = left_end
        for t in range(4):
            strip = ensemble[8 * t : 8 * (t + 1), LANES:]
            swapped = pltpu.roll(strip, 4, 0)
            inside = jnp.logical_and(lane >= GAP * t, lane < GAP * (t + 1))
            left_end = jnp.where(inside, pltpu.roll(strip, (GAP * t - EDGE) % LANES, 1), left_end)
            if t < 3:
                right_end = jnp.where(inside, pltpu.roll(swapped, (GAP * t - EDGE) % LANES, 1), right_end)
            else:
                left_end = jnp.where(lane >= 4 * GAP, pltpu.roll(swapped, LANES - EDGE - 4, 1), left_end)
                right_end = jnp.where(lane >= 3 * GAP, pltpu.roll(swapped, LANES + 3 * GAP - EDGE - 4, 1), right_end)
        ensemble = jnp.concatenate([ensemble, jnp.concatenate([left_end, right_end], axis=1)], axis=0)
        for f in range(HALF):
            field = ensemble[:, WIDTH * f : WIDTH * (f + 1)] + static_ext[s * HALF + f]
            state[s * HALF + f, :, STEPS : STEPS + WIDTH] = field
            inc_out[s * HALF + f] = field[STEPS : STEPS + ROWS, :]
    for side, low in enumerate((STEPS, WIDTH)):
        edge_send[side] = jnp.concatenate([state[f, :, low : low + STEPS] for f in range(FIELDS)], axis=1)
    edge_west = remote(edge_send.at[0], edge_recv.at[1], edge_ssem.at[0], edge_rsem.at[1], at(i, west))
    edge_east = remote(edge_send.at[1], edge_recv.at[0], edge_ssem.at[1], edge_rsem.at[0], at(i, east))
    edge_west.start()
    edge_east.start()

    for send in (ring, lat_ring):
        for slot in range(4):
            send(0, up_send, up_recv, slot, up_dev).wait_send()
        for slot in range(3):
            send(0, down_send, down_recv, slot, down_dev).wait_send()

    def twins(k, carry):
        across(0, k).wait_send()
        lat_across(0, k).wait_send()

        @pl.when(k != zl)
        def _():
            for copy in beside(0, (quarter, quarter, quarter), k):
                copy.wait_send()
            lat_beside(0, half, k).wait_send()

        return carry

    lax.fori_loop(0, ZLO, twins, 0)

    def packs(p, carry):
        for hh in range(ZHI):
            for cc in range(CORES):
                mine = jnp.logical_and(p == xy, jnp.logical_and(h == hh, c == cc))

                @pl.when(jnp.logical_not(mine))
                def _():
                    remote(
                        packed.at[p, hh, cc], spread.at[0, 0], pack_send.at[p, hh, cc], pack_recv.at[0, 0], twin_dev
                    ).wait_send()

        return carry

    lax.fori_loop(0, MEM, packs, 0)

    def totals(k, carry):
        @pl.when(k != i)
        def _():
            remote(sum_send.at[k], sum_recv.at[0], total_send.at[k], total_recv.at[0], twin_dev).wait_send()

        return carry

    lax.fori_loop(0, MEM, totals, 0)

    edge_west.wait()
    edge_east.wait()
    u, v = wind[0], wind[1]
    u_pos, u_neg = jnp.maximum(u, 0.0), jnp.minimum(u, 0.0)
    v_pos, v_neg = jnp.maximum(v, 0.0), jnp.minimum(v, 0.0)
    for f in range(FIELDS):
        state[f, :, :STEPS] = edge_recv[0, :, STEPS * f : STEPS * (f + 1)]
        state[f, :, STEPS + WIDTH : 2 * STEPS + WIDTH] = edge_recv[1, :, STEPS * f : STEPS * (f + 1)]

    def advance(f, carry):
        q = state[f]
        for _ in range(STEPS):
            western = pltpu.roll(q, 1, 1)
            eastern = pltpu.roll(q, q.shape[1] - 1, 1)
            southern = pltpu.roll(q, 1, 0)
            northern = pltpu.roll(q, q.shape[0] - 1, 0)
            zonal = u_pos * (q - western) + u_neg * (eastern - q)
            meridional = v_pos * (q - southern) + v_neg * (northern - q)
            q = q - zonal - meridional
        evo_out[f] = q[STEPS : STEPS + ROWS, STEPS : STEPS + WIDTH]
        return carry

    lax.fori_loop(0, FIELDS, advance, 0)


def per_device(control, perturb, lon_loc, lat_loc, static_scale, static_field, courant):
    anywhere = pl.BlockSpec(memory_space=pl.ANY)
    vmem = pl.BlockSpec(memory_space=pltpu.VMEM)
    bf16, f32 = jnp.bfloat16, jnp.float32
    dma = pltpu.SemaphoreType.DMA
    out = jax.ShapeDtypeStruct((FIELDS, ROWS, WIDTH), f32)
    return pl.pallas_call(
        kernel,
        out_shape=(out, out),
        in_specs=[anywhere] * 2 + [vmem] * 5,
        out_specs=(vmem, vmem),
        scratch_shapes=[
            pltpu.VMEM((FIELDS, BAND, LOCAL, NLON), bf16),
            pltpu.VMEM((LOCAL * FIELDS, BAND_PAD, NLON), bf16),
            pltpu.VMEM((FIELDS, WIDTH, LOCAL, NLAT), bf16),
            pltpu.VMEM((CORES, PACKED, NLAT), bf16),
            pltpu.VMEM((PACKED, NLAT), bf16),
            pltpu.VMEM((MEM, QUARTERS, BAND_PAD, NLON), bf16),
            pltpu.VMEM((MEM, 2, BAND_PAD, NLAT), bf16),
            pltpu.VMEM((XY, ZHI, CORES, WIRE_ROWS, LANES), bf16),
            pltpu.VMEM((CORES, LAT, WIRE_ROWS, LANES), bf16),
            pltpu.VMEM((MEM, ROWS_PAD, NLAT), bf16),
            pltpu.VMEM((2, EXPANDED // 2, LAT * BAND_PAD), bf16),
            pltpu.VMEM((2, CORES, EXPANDED // 2, PACKED), bf16),
            pltpu.VMEM((CORES, LAT, BAND_PAD, LANES), bf16),
            pltpu.VMEM((MEM, SENT_ROWS, 2 * LANES), bf16),
            pltpu.VMEM((MEM, SENT_ROWS, 2 * LANES), bf16),
            pltpu.VMEM((2, FIELDS + 2, 8, WIDTH), f32),
            pltpu.VMEM((2, FIELDS + 2, 8, WIDTH), f32),
            pltpu.VMEM((FIELDS, ROWS_PAD, WIDTH), f32),
            pltpu.VMEM((2, ROWS_PAD, 128), f32),
            pltpu.VMEM((2, ROWS_PAD, 2 * STEPS), f32),
            pltpu.VMEM((2, ROWS_PAD, 2 * STEPS), f32),
            pltpu.VMEM((FIELDS, ROWS_PAD, 128), f32),
            pltpu.VMEM((2, ROWS_PAD, FIELDS * STEPS), f32),
            pltpu.VMEM((2, ROWS_PAD, FIELDS * STEPS), f32),
            dma((4,)), dma((2, 4)), dma((2, 4)), dma((2, 3)), dma((2, 3)), dma((4, ZLO)), dma((4, ZLO)),
            dma((2, ZLO)), dma((2, ZLO)),
            dma((1,)), dma((1,)), dma((XY, ZHI, CORES)), dma((CORES, LAT)), dma((MEM,)), dma((MEM,)),
            dma((2,)), dma((2,)), dma((2,)), dma((2,)), dma((2,)), dma((2,)),
        ],
        compiler_params=pltpu.CompilerParams(
            collective_id=0, has_side_effects=True, vmem_limit_bytes=56 * 1024 * 1024
        ),
        name="increment",
    )(
        control.transpose(1, 2, 0, 3),
        perturb.transpose(1, 3, 0, 2),
        lon_loc.T,
        lat_loc,
        static_scale,
        static_field,
        courant.transpose(1, 0, 2),
    )


def solution(mesh):
    placed = (
        P("mem", None, "lat", None),
        P("mem", None, None, "lat"),
        P(None, "mem"),
        P("mem", None),
        P(None, "mem", "lat"),
        P(None, "mem", "lat"),
        P(None, "mem", "lat"),
    )
    return jax.shard_map(
        per_device,
        mesh=mesh,
        in_specs=placed,
        out_specs=(P(None, "mem", "lat"), P(None, "mem", "lat")),
        check_vma=False,
    )
```

```python
import functools
import math

import jax
import jax.numpy as jnp
from jax import lax
from jax.experimental import pallas as pl
from jax.experimental.pallas import tpu as pltpu
from jax.sharding import PartitionSpec as P

STEPS = 4
ZLO = 8
CORES = 2
XY = 16
ZHI = 2
MEM = ZLO * CORES
LAT = XY * ZHI
FIELDS = 10
HALF = FIELDS // 2
LOCAL = 2
NLAT = 704
NLON = 1440
BAND = NLAT // LAT
BAND_PAD = 24
WIDTH = NLON // LAT
ROWS = NLAT // MEM
ROWS_EXT = ROWS + 2 * STEPS
ROWS_PAD = 56
LON_BLOCK = NLON // MEM
LAT_BLOCK = 2 * BAND_PAD
QUARTERS = 4
LANES = 128
WHOLE = 3 * LANES
REST = LOCAL * HALF * WIDTH - WHOLE
FOLD = LANES - REST
WIRE_ROWS = 3 * BAND_PAD + 8
SPARE = REST - FOLD
SENT_ROWS = 48
EDGE = HALF * WIDTH - LANES
GAP = LANES - EDGE
PACKED = LOCAL * HALF * WIDTH
SUMMED = HALF * WIDTH
EXPANDED = MEM * ROWS_PAD
RELAY_AT = (1, 4, 8, 12)
COMPLETE_AT = (2, 6, 10, 14)
LAT_AT = (5, 7, 11, 13)
MESH = pl.DeviceIdType.MESH
SCALE = 1.0 / math.sqrt(31.0)
NT = (((1,), (1,)), ((), ()))
NN = (((1,), (0,)), ((), ()))


def matmul(a, b, dims):
    return lax.dot_general(a, b, dims, preferred_element_type=jnp.float32)


def kernel(
    control_hbm, perturb_hbm, lon_ref, lat_ref, scale_ref, field_ref, courant_ref,
    inc_out, evo_out,
    control_raw, control, members_raw, members, gift, lon_all, lat_all, packed, spread, expand, lat_t, pert_t,
    rest, sum_send, sum_recv, rows_send, rows_recv, static_ext, wind, wind_send, wind_recv,
    state, edge_send, edge_recv,
    local_sem, up_send, up_recv, down_send, down_recv, side_send, side_recv, twin_send, twin_recv,
    mem_send, mem_recv, pack_send, pack_recv, total_send, total_recv,
    rim_send, rim_recv, wind_ssem, wind_rsem, edge_ssem, edge_rsem,
):
    i = lax.axis_index("mem")
    j = lax.axis_index("lat")
    zl, c = i // 2, i % 2
    xy, h = j // 2, j % 2
    x, y = xy // 4, xy % 4
    half = (x + y) % 2
    quarter = 2 * (x % 2) + y % 2
    quarter_x, quarter_y = 2 - 2 * (x % 2) + y % 2, 2 * (x % 2) + 1 - y % 2
    lag = 1 + xy % 8
    next_x, next_y = (x + 1 + 2 * c) % 4, (y + 1 + 2 * c) % 4
    twin = 2 * zl + 1 - c
    above = (h * ZLO + zl + 1) % 16
    below = (h * ZLO + zl + 15) % 16

    def at(mem, lat):
        return {"mem": mem, "lat": lat}

    up_dev = at(2 * (above % ZLO) + c, 2 * xy + above // ZLO)
    down_dev = at(2 * (below % ZLO) + c, 2 * xy + below // ZLO)
    twin_dev = at(twin, j)
    x_dev = at(i, 2 * (4 * next_x + y) + h)
    y_dev = at(i, 2 * (4 * x + next_y) + h)
    diagonal_dev = at(i, 2 * (4 * next_x + next_y) + h)

    def remote(src, dst, ssem, rsem, dev):
        return pltpu.make_async_remote_copy(
            src_ref=src, dst_ref=dst, send_sem=ssem, recv_sem=rsem,
            device_id=dev, device_id_type=MESH,
        )

    get_control = pltpu.make_async_copy(control_hbm, control_raw, local_sem.at[0])
    get_members = pltpu.make_async_copy(perturb_hbm, members_raw, local_sem.at[1])
    get_control.start()
    get_members.start()

    barrier = pltpu.get_barrier_semaphore()

    def greet(mem, lat):
        pl.semaphore_signal(barrier, inc=1, device_id=at(mem, lat), device_id_type=MESH)

    greet(2 * (above % ZLO) + c, 2 * xy + above // ZLO)
    greet(2 * (below % ZLO) + c, 2 * xy + below // ZLO)
    greet(twin, j)

    def greet_lat(k, carry):
        other = (j + k) % LAT
        greet(i, other)
        greet(twin, other)
        return carry

    lax.fori_loop(1, LAT, greet_lat, 0)

    def greet_mem(k, carry):
        other = (zl + k) % ZLO
        greet(2 * other, j)
        greet(2 * other + 1, j)
        return carry

    lax.fori_loop(1, ZLO, greet_mem, 0)
    for q in range(QUARTERS):
        held = lon_ref[BAND_PAD * q : min(BAND_PAD * (q + 1), LON_BLOCK), :].astype(jnp.float32)
        if held.shape[0] < BAND_PAD:
            held = jnp.concatenate([held, jnp.zeros((BAND_PAD - held.shape[0], NLON), jnp.float32)], axis=0)
        lon_all[i, q] = held.astype(jnp.bfloat16)
    lat_rows = lat_ref[...].astype(jnp.float32)
    for b in range(2):
        held = jnp.concatenate(
            [lat_rows[BAND * b : BAND * (b + 1)], jnp.zeros((BAND_PAD - BAND, NLAT), jnp.float32)], axis=0
        )
        lat_all[i, b] = held.astype(jnp.bfloat16)
    product = scale_ref[...] * field_ref[...]
    static_ext[:, STEPS : STEPS + ROWS, :] = product
    rows_send[0, :FIELDS] = product[:, :8, :]
    rows_send[1, :FIELDS] = product[:, ROWS - 8 :, :]
    for k in range(2):
        rows_send[0, FIELDS + k] = courant_ref[:8, k, :]
        rows_send[1, FIELDS + k] = courant_ref[ROWS - 8 :, k, :]
    first_row, last_row = i == 0, i == MEM - 1

    @pl.when(first_row)
    def _():
        rows_recv[0] = jnp.zeros(rows_recv.shape[1:], rows_recv.dtype)

    @pl.when(last_row)
    def _():
        rows_recv[1] = jnp.zeros(rows_recv.shape[1:], rows_recv.dtype)

    get_control.wait()

    def place(f, carry):
        held = control_raw[f].astype(jnp.float32)
        for m in range(LOCAL):
            rows = jnp.concatenate([held[:, m, :], jnp.zeros((BAND_PAD - BAND, NLON), jnp.float32)], axis=0)
            control[m * FIELDS + f] = rows.astype(jnp.bfloat16)
        return carry

    lax.fori_loop(0, FIELDS, place, 0)

    pl.semaphore_wait(barrier, 3 + 2 * (LAT - 1) + 2 * (ZLO - 1))

    def ring(p, send, recv, slot, dev):
        part = lon_all.at[p, quarter]
        return remote(part, part, send.at[0, slot], recv.at[0, slot], dev)

    def lat_ring(p, send, recv, slot, dev):
        part = lat_all.at[p, half]
        return remote(part, part, send.at[1, slot], recv.at[1, slot], dev)

    def beside(p, parts, slot):
        return [
            remote(lon_all.at[p, part], lon_all.at[p, part], side_send.at[k, slot], side_recv.at[k, slot], dev)
            for k, (part, dev) in enumerate(zip(parts, (x_dev, y_dev, diagonal_dev)))
        ]

    def lat_beside(p, part, slot):
        part = lat_all.at[p, part]
        return remote(part, part, side_send.at[3, slot], side_recv.at[3, slot], x_dev)

    def across(p, slot):
        return remote(lon_all.at[p], lon_all.at[p], twin_send.at[0, slot], twin_recv.at[0, slot], twin_dev)

    def lat_across(p, slot):
        return remote(lat_all.at[p], lat_all.at[p], twin_send.at[1, slot], twin_recv.at[1, slot], twin_dev)

    def start(copies):
        for copy in copies:
            copy.start()

    ring(i, up_send, up_recv, 0, up_dev).start()
    ring(i, down_send, down_recv, 0, down_dev).start()
    across(i, zl).start()

    to_before = remote(rows_send.at[0], rows_recv.at[1], rim_send.at[0], rim_recv.at[1], at(jnp.maximum(i - 1, 0), j))
    to_after = remote(rows_send.at[1], rows_recv.at[0], rim_send.at[1], rim_recv.at[0], at(jnp.minimum(i + 1, MEM - 1), j))
    give_members = remote(
        gift, members.at[c], mem_send.at[0], mem_recv.at[0], twin_dev
    )

    def relay(d, ring, share):
        source = (zl + ZLO - d) % ZLO
        ring(2 * source + c, up_send, up_recv, d - 1, up_dev).wait_recv()
        if d < 4:
            ring(2 * source + c, up_send, up_recv, d, up_dev).start()
        share(2 * source + c, source)
        if d < 4:
            source = (zl + d) % ZLO
            ring(2 * source + c, down_send, down_recv, d - 1, down_dev).wait_recv()
            if d < 3:
                ring(2 * source + c, down_send, down_recv, d, down_dev).start()
            share(2 * source + c, source)

    def complete(d):
        for step in (-1, 1) if d < 4 else (-1,):
            source = (zl + ZLO + step * d) % ZLO
            for copy in beside(2 * source + c, (quarter_x, quarter_y, 3 - quarter), source):
                copy.wait_recv()
            across(2 * source + c, source).start()

    def chosen(n):
        d = (n + 2) // 4
        r = (n + 2) % 4
        middle = (d + 3) // 4 - d // 4
        other = middle * (r // 2) + (1 - middle) * (r % 2)
        downward = middle * (r % 2)
        source = (zl + d * (2 * downward - 1) + ZLO) % ZLO
        return 2 * source + (c + other) % 2, source, other

    def near(n):
        p, _, _ = chosen(n)
        for cc in range(CORES):
            mine = jnp.logical_and(p == xy, c == cc)

            @pl.when(mine)
            def _():
                pltpu.make_async_copy(packed.at[p, h, cc], spread.at[c, j], pack_recv.at[c, j]).start()

            @pl.when(jnp.logical_not(mine))
            def _():
                remote(
                    packed.at[p, h, cc], spread.at[c, j], pack_send.at[p, h, cc], pack_recv.at[c, j],
                    at(2 * zl + cc, 2 * p + h),
                ).start()

    west, east = (j + LAT - 1) % LAT, (j + 1) % LAT
    wind_west = remote(wind_send.at[0], wind_recv.at[1], wind_ssem.at[0], wind_rsem.at[1], at(i, west))
    wind_east = remote(wind_send.at[1], wind_recv.at[0], wind_ssem.at[1], wind_rsem.at[0], at(i, east))

    def member_rows(part):
        rows = [members_raw[part * HALF + f].astype(jnp.float32)[:, m, :] for m in range(LOCAL) for f in range(HALF)]
        return jnp.concatenate(rows, axis=0).astype(jnp.bfloat16)

    def share_members():
        get_members.wait()
        gift[...] = member_rows(1 - c)
        give_members.start()
        members[c] = member_rows(c)

    def share_wind():
        @pl.when(jnp.logical_not(first_row))
        def _():
            to_after.wait_recv()
            to_before.wait_send()

        @pl.when(jnp.logical_not(last_row))
        def _():
            to_before.wait_recv()
            to_after.wait_send()

        static_ext[:, :STEPS, :] = rows_recv[0, :FIELDS, 8 - STEPS :, :]
        static_ext[:, STEPS + ROWS : ROWS_EXT, :] = rows_recv[1, :FIELDS, :STEPS, :]
        static_ext[:, ROWS_EXT:, :] = jnp.zeros((FIELDS, ROWS_PAD - ROWS_EXT, WIDTH), jnp.float32)
        wind[...] = jnp.zeros_like(wind)
        wind[:, :STEPS, STEPS : STEPS + WIDTH] = rows_recv[0, FIELDS:, 8 - STEPS :, :]
        for k in range(2):
            wind[k, STEPS : STEPS + ROWS, STEPS : STEPS + WIDTH] = courant_ref[:, k, :]
        wind[:, STEPS + ROWS : ROWS_EXT, STEPS : STEPS + WIDTH] = rows_recv[1, FIELDS:, :STEPS, :]
        for side, low in enumerate((STEPS, WIDTH)):
            wind_send[side] = jnp.concatenate([wind[k, :, low : low + STEPS] for k in range(2)], axis=1)
        wind_west.start()
        wind_east.start()

    def block(n, carry):
        p, source, other = chosen(n)

        for d in range(1, 5):

            @pl.when(n == RELAY_AT[d - 1])
            def _():
                relay(d, ring, lambda p, k: start(beside(p, (quarter, quarter, quarter), k)))

            @pl.when(n == COMPLETE_AT[d - 1])
            def _():
                complete(d)

            @pl.when(n == LAT_AT[d - 1])
            def _():
                if d == 1:
                    lat_ring(i, up_send, up_recv, 0, up_dev).start()
                    lat_ring(i, down_send, down_recv, 0, down_dev).start()
                    lat_across(i, zl).start()
                else:
                    relay(d - 1, lat_ring, lambda p, k: lat_beside(p, half, k).start())

        @pl.when(other == 1)
        def _():
            across(p, source).wait_recv()

        lon_rows = lon_all[p].reshape(QUARTERS * BAND_PAD, NLON)
        along = matmul(control[...].reshape(LOCAL * FIELDS * BAND_PAD, NLON), lon_rows, NT)
        lane = lax.broadcasted_iota(jnp.int32, (8, LANES), 1)
        sub = lax.broadcasted_iota(jnp.int32, (8, LANES), 0)
        for hh in range(ZHI):
            for cc in range(CORES):
                pieces = [
                    along[
                        BAND_PAD * (m * FIELDS + cc * HALF + f) : BAND_PAD * (m * FIELDS + cc * HALF + f + 1),
                        WIDTH * hh : WIDTH * (hh + 1),
                    ]
                    for m in range(LOCAL)
                    for f in range(HALF)
                ]
                pieces.append(jnp.zeros((BAND_PAD, FOLD), jnp.float32))
                row = jnp.concatenate(pieces, axis=1)
                last = row[:, WHOLE:]
                low, middle_rows, high = last[:8], last[8:16], last[16:]
                folded = jnp.where(lane < REST, low, pltpu.roll(middle_rows, REST, 1))
                wire = []
                for t in range(3):
                    tile = row[:, LANES * t : LANES * (t + 1)]
                    spare = jnp.where(lane < REST, pltpu.roll(high, 6 - 2 * t, 0), 0.0)
                    if t == 0:
                        for e in range(4):
                            start_lane = REST + SPARE * e
                            moved = pltpu.roll(pltpu.roll(middle_rows, start_lane - FOLD, 1), (6 - 2 * e) % 8, 0)
                            inside = jnp.logical_and(lane >= start_lane, lane < start_lane + SPARE)
                            spare = jnp.where(inside, moved, spare)
                    wire += [tile[:16], jnp.where(sub < 6, tile[16:], spare)]
                wire.append(folded)
                packed[p, hh, cc] = jnp.concatenate(wire, axis=0).astype(jnp.bfloat16)
        for cc in range(CORES):
            remote(
                packed.at[p, 1 - h, cc], spread.at[c, j], pack_send.at[p, 1 - h, cc], pack_recv.at[c, j],
                at(2 * zl + cc, 2 * p + 1 - h),
            ).start()

        @pl.when(n >= lag)
        def _():
            near(n - lag)

        @pl.when(n == 1)
        def _():
            @pl.when(jnp.logical_not(first_row))
            def _():
                to_before.start()

            @pl.when(jnp.logical_not(last_row))
            def _():
                to_after.start()

        @pl.when(n == 9)
        def _():
            share_wind()

        @pl.when(n == 11)
        def _():
            share_members()

        return carry

    lax.fori_loop(0, MEM, block, 0)

    def late(k, carry):
        near(MEM - lag + k)
        return carry

    lax.fori_loop(0, lag, late, 0)

    relay(4, lat_ring, lambda p, k: lat_beside(p, half, k).start())
    def select_rows(k, carry):
        row = lax.broadcasted_iota(jnp.int32, (ROWS_PAD, NLAT), 0)
        col = lax.broadcasted_iota(jnp.int32, (ROWS_PAD, NLAT), 1)
        hit = jnp.logical_and(col == row + (ROWS * k - STEPS), row < ROWS_EXT)
        expand[k] = jnp.where(hit, 1.0, 0.0).astype(jnp.bfloat16)
        return carry

    lax.fori_loop(0, MEM, select_rows, 0)

    def lat_complete(k, carry):
        @pl.when(k != zl)
        def _():
            lat_beside(2 * k + c, 1 - half, k).wait_recv()
            lat_across(2 * k + c, k).start()

        return carry

    lax.fori_loop(0, ZLO, lat_complete, 0)

    def lat_arrived(k, carry):
        lat_across(2 * k + 1 - c, k).wait_recv()
        return carry

    lax.fori_loop(0, ZLO, lat_arrived, 0)
    lat_flat = lat_all[...].reshape(MEM * LAT_BLOCK, NLAT)
    rows_half = EXPANDED // 2
    for part in range(2):
        chooser = expand[part * ZLO : (part + 1) * ZLO].reshape(rows_half, NLAT)
        lat_t[part] = matmul(chooser, lat_flat, NT).astype(jnp.bfloat16)
    give_members.wait()
    for part in range(2):
        chooser = expand[part * ZLO : (part + 1) * ZLO].reshape(rows_half, NLAT)
        for s in range(CORES):
            pert_t[part, s] = matmul(chooser, members[s], NT).astype(jnp.bfloat16)

    wind_west.wait()
    wind_east.wait()
    for k in range(2):
        wind[k, :, :STEPS] = wind_recv[0, :, STEPS * k : STEPS * (k + 1)]
        wind[k, :, STEPS + WIDTH : 2 * STEPS + WIDTH] = wind_recv[1, :, STEPS * k : STEPS * (k + 1)]

    lane = lax.broadcasted_iota(jnp.int32, (8, LANES), 1)
    sub = lax.broadcasted_iota(jnp.int32, (8, LANES), 0)

    def arrived(k, carry):
        for s in range(CORES):
            remote(packed.at[0, 0, 0], spread.at[s, k], pack_send.at[0, 0, 0], pack_recv.at[s, k], twin_dev).wait_recv()
            folded = spread[s, k, 3 * BAND_PAD :, :].astype(jnp.float32)
            middle_rows = pltpu.roll(folded, FOLD, 1)
            high = jnp.zeros((8, LANES), jnp.float32)
            for t in range(3):
                spare = spread[s, k, BAND_PAD * t + 16 : BAND_PAD * (t + 1), :].astype(jnp.float32)
                pair = jnp.logical_and(sub >= 2 * t, sub < 2 * t + 2)
                high = jnp.where(pair, pltpu.roll(spare, (2 * t + 2) % 8, 0), high)
                if t == 0:
                    for e in range(4):
                        shift = (FOLD - REST - SPARE * e) % LANES
                        moved = pltpu.roll(pltpu.roll(spare, shift, 1), (2 * e + 2) % 8, 0)
                        inside = jnp.logical_and(sub >= 2 * e, sub < 2 * e + 2)
                        middle_rows = jnp.where(jnp.logical_and(inside, lane >= FOLD), moved, middle_rows)
            rest[s, k] = jnp.concatenate([folded, middle_rows, high], axis=0).astype(jnp.bfloat16)
        return carry

    lax.fori_loop(0, LAT, arrived, 0)
    for part in range(2):
        total = None
        for s in range(CORES):
            tiles = [spread[s, :, BAND_PAD * t : BAND_PAD * (t + 1), :] for t in range(3)] + [rest[s]]
            tiles = [t.reshape(LAT * BAND_PAD, LANES) for t in tiles]
            term = matmul(lat_t[part], jnp.concatenate(tiles, axis=1), NN)[:, :PACKED]
            term = term * pert_t[part, s].astype(jnp.float32)
            total = term if total is None else total + term
        summed = (total[:, :SUMMED] + total[:, SUMMED:]) * SCALE
        summed = jnp.concatenate([summed, jnp.zeros((rows_half, GAP), jnp.float32)], axis=1)
        for k in range(ZLO):
            chunk = summed[ROWS_PAD * k : ROWS_PAD * (k + 1)]
            right = chunk[:, LANES:]
            left_end, right_end = chunk[SENT_ROWS:, :LANES], right[SENT_ROWS:]
            strips = []
            for t in range(SENT_ROWS // 8):
                strip = right[8 * t : 8 * (t + 1)]
                if t < 4:
                    if t < 3:
                        second = pltpu.roll(right_end, EDGE - GAP * t, 1)
                    else:
                        second = jnp.where(
                            lane < EDGE + 4,
                            pltpu.roll(left_end, EDGE + 4, 1),
                            pltpu.roll(right_end, EDGE + 4 - 3 * GAP, 1),
                        )
                    first = pltpu.roll(left_end, (EDGE - GAP * t) % LANES, 1)
                    spare = jnp.where(sub < 4, first, pltpu.roll(second, 4, 0))
                    strip = jnp.where(lane < EDGE, strip, spare)
                strips.append(strip)
            sent = jnp.concatenate([chunk[:SENT_ROWS, :LANES], jnp.concatenate(strips, axis=0)], axis=1)
            sum_send[part * ZLO + k] = sent.astype(jnp.bfloat16)

        def give(k, carry):
            for step in (1, -1):
                other = zl + step * (ZLO - 1 - k)

                @pl.when(jnp.logical_and(other >= part * (ZLO // 2), other < (part + 1) * (ZLO // 2)))
                def _():
                    for cc in range(CORES):
                        owner = 2 * other + cc
                        remote(
                            sum_send.at[owner], sum_recv.at[i], total_send.at[owner], total_recv.at[i], at(owner, j)
                        ).start()

            return carry

        lax.fori_loop(0, ZLO - 1, give, 0)

    pltpu.make_async_copy(sum_send.at[i], sum_recv.at[i], total_recv.at[i]).start()
    remote(sum_send.at[twin], sum_recv.at[i], total_send.at[twin], total_recv.at[i], twin_dev).start()

    def gathered(k, carry):
        remote(sum_send.at[0], sum_recv.at[k], total_send.at[0], total_recv.at[k], twin_dev).wait_recv()
        return carry

    lax.fori_loop(0, MEM, gathered, 0)
    state[...] = jnp.zeros_like(state)
    for s in range(CORES):
        ensemble = sum_recv[s].astype(jnp.float32)
        for z in range(1, ZLO):
            ensemble = ensemble + sum_recv[CORES * z + s].astype(jnp.float32)
        left_end = jnp.zeros((8, LANES), jnp.float32)
        right_end = left_end
        for t in range(4):
            strip = ensemble[8 * t : 8 * (t + 1), LANES:]
            swapped = pltpu.roll(strip, 4, 0)
            inside = jnp.logical_and(lane >= GAP * t, lane < GAP * (t + 1))
            left_end = jnp.where(inside, pltpu.roll(strip, (GAP * t - EDGE) % LANES, 1), left_end)
            if t < 3:
                right_end = jnp.where(inside, pltpu.roll(swapped, (GAP * t - EDGE) % LANES, 1), right_end)
            else:
                left_end = jnp.where(lane >= 4 * GAP, pltpu.roll(swapped, LANES - EDGE - 4, 1), left_end)
                right_end = jnp.where(lane >= 3 * GAP, pltpu.roll(swapped, LANES + 3 * GAP - EDGE - 4, 1), right_end)
        ensemble = jnp.concatenate([ensemble, jnp.concatenate([left_end, right_end], axis=1)], axis=0)
        for f in range(HALF):
            field = ensemble[:, WIDTH * f : WIDTH * (f + 1)] + static_ext[s * HALF + f]
            state[s * HALF + f, :, STEPS : STEPS + WIDTH] = field
            inc_out[s * HALF + f] = field[STEPS : STEPS + ROWS, :]
    for side, low in enumerate((STEPS, WIDTH)):
        edge_send[side] = jnp.concatenate([state[f, :, low : low + STEPS] for f in range(FIELDS)], axis=1)
    edge_west = remote(edge_send.at[0], edge_recv.at[1], edge_ssem.at[0], edge_rsem.at[1], at(i, west))
    edge_east = remote(edge_send.at[1], edge_recv.at[0], edge_ssem.at[1], edge_rsem.at[0], at(i, east))
    edge_west.start()
    edge_east.start()

    for send in (ring, lat_ring):
        for slot in range(4):
            send(0, up_send, up_recv, slot, up_dev).wait_send()
        for slot in range(3):
            send(0, down_send, down_recv, slot, down_dev).wait_send()

    def twins(k, carry):
        across(0, k).wait_send()
        lat_across(0, k).wait_send()

        @pl.when(k != zl)
        def _():
            for copy in beside(0, (quarter, quarter, quarter), k):
                copy.wait_send()
            lat_beside(0, half, k).wait_send()

        return carry

    lax.fori_loop(0, ZLO, twins, 0)

    def packs(p, carry):
        for hh in range(ZHI):
            for cc in range(CORES):
                mine = jnp.logical_and(p == xy, jnp.logical_and(h == hh, c == cc))

                @pl.when(jnp.logical_not(mine))
                def _():
                    remote(
                        packed.at[p, hh, cc], spread.at[0, 0], pack_send.at[p, hh, cc], pack_recv.at[0, 0], twin_dev
                    ).wait_send()

        return carry

    lax.fori_loop(0, MEM, packs, 0)

    def totals(k, carry):
        @pl.when(k != i)
        def _():
            remote(sum_send.at[k], sum_recv.at[0], total_send.at[k], total_recv.at[0], twin_dev).wait_send()

        return carry

    lax.fori_loop(0, MEM, totals, 0)

    edge_west.wait()
    edge_east.wait()
    u, v = wind[0], wind[1]
    u_pos, u_neg = jnp.maximum(u, 0.0), jnp.minimum(u, 0.0)
    v_pos, v_neg = jnp.maximum(v, 0.0), jnp.minimum(v, 0.0)
    for f in range(FIELDS):
        state[f, :, :STEPS] = edge_recv[0, :, STEPS * f : STEPS * (f + 1)]
        state[f, :, STEPS + WIDTH : 2 * STEPS + WIDTH] = edge_recv[1, :, STEPS * f : STEPS * (f + 1)]

    def advance(f, carry):
        q = state[f]
        for _ in range(STEPS):
            western = pltpu.roll(q, 1, 1)
            eastern = pltpu.roll(q, q.shape[1] - 1, 1)
            southern = pltpu.roll(q, 1, 0)
            northern = pltpu.roll(q, q.shape[0] - 1, 0)
            zonal = u_pos * (q - western) + u_neg * (eastern - q)
            meridional = v_pos * (q - southern) + v_neg * (northern - q)
            q = q - zonal - meridional
        evo_out[f] = q[STEPS : STEPS + ROWS, STEPS : STEPS + WIDTH]
        return carry

    lax.fori_loop(0, FIELDS, advance, 0)


def per_device(control, perturb, lon_loc, lat_loc, static_scale, static_field, courant):
    anywhere = pl.BlockSpec(memory_space=pl.ANY)
    vmem = pl.BlockSpec(memory_space=pltpu.VMEM)
    bf16, f32 = jnp.bfloat16, jnp.float32
    dma = pltpu.SemaphoreType.DMA
    out = jax.ShapeDtypeStruct((FIELDS, ROWS, WIDTH), f32)
    return pl.pallas_call(
        kernel,
        out_shape=(out, out),
        in_specs=[anywhere] * 2 + [vmem] * 5,
        out_specs=(vmem, vmem),
        scratch_shapes=[
            pltpu.VMEM((FIELDS, BAND, LOCAL, NLON), bf16),
            pltpu.VMEM((LOCAL * FIELDS, BAND_PAD, NLON), bf16),
            pltpu.VMEM((FIELDS, WIDTH, LOCAL, NLAT), bf16),
            pltpu.VMEM((CORES, PACKED, NLAT), bf16),
            pltpu.VMEM((PACKED, NLAT), bf16),
            pltpu.VMEM((MEM, QUARTERS, BAND_PAD, NLON), bf16),
            pltpu.VMEM((MEM, 2, BAND_PAD, NLAT), bf16),
            pltpu.VMEM((XY, ZHI, CORES, WIRE_ROWS, LANES), bf16),
            pltpu.VMEM((CORES, LAT, WIRE_ROWS, LANES), bf16),
            pltpu.VMEM((MEM, ROWS_PAD, NLAT), bf16),
            pltpu.VMEM((2, EXPANDED // 2, LAT * BAND_PAD), bf16),
            pltpu.VMEM((2, CORES, EXPANDED // 2, PACKED), bf16),
            pltpu.VMEM((CORES, LAT, BAND_PAD, LANES), bf16),
            pltpu.VMEM((MEM, SENT_ROWS, 2 * LANES), bf16),
            pltpu.VMEM((MEM, SENT_ROWS, 2 * LANES), bf16),
            pltpu.VMEM((2, FIELDS + 2, 8, WIDTH), f32),
            pltpu.VMEM((2, FIELDS + 2, 8, WIDTH), f32),
            pltpu.VMEM((FIELDS, ROWS_PAD, WIDTH), f32),
            pltpu.VMEM((2, ROWS_PAD, 128), f32),
            pltpu.VMEM((2, ROWS_PAD, 2 * STEPS), f32),
            pltpu.VMEM((2, ROWS_PAD, 2 * STEPS), f32),
            pltpu.VMEM((FIELDS, ROWS_PAD, 128), f32),
            pltpu.VMEM((2, ROWS_PAD, FIELDS * STEPS), f32),
            pltpu.VMEM((2, ROWS_PAD, FIELDS * STEPS), f32),
            dma((4,)), dma((2, 4)), dma((2, 4)), dma((2, 3)), dma((2, 3)), dma((4, ZLO)), dma((4, ZLO)),
            dma((2, ZLO)), dma((2, ZLO)),
            dma((1,)), dma((1,)), dma((XY, ZHI, CORES)), dma((CORES, LAT)), dma((MEM,)), dma((MEM,)),
            dma((2,)), dma((2,)), dma((2,)), dma((2,)), dma((2,)), dma((2,)),
        ],
        compiler_params=pltpu.CompilerParams(
            collective_id=0, has_side_effects=True, vmem_limit_bytes=56 * 1024 * 1024
        ),
        name="increment",
    )(
        control.transpose(1, 2, 0, 3),
        perturb.transpose(1, 3, 0, 2),
        lon_loc.T,
        lat_loc,
        static_scale,
        static_field,
        courant.transpose(1, 0, 2),
    )


def solution(mesh):
    placed = (
        P("mem", None, "lat", None),
        P("mem", None, None, "lat"),
        P(None, "mem"),
        P("mem", None),
        P(None, "mem", "lat"),
        P(None, "mem", "lat"),
        P(None, "mem", "lat"),
    )
    return jax.shard_map(
        per_device,
        mesh=mesh,
        in_specs=placed,
        out_specs=(P(None, "mem", "lat"), P(None, "mem", "lat")),
        check_vma=False,
    )
```
